512 devices in a mesh: ctx: 64 (over x, z_lo, y), head: 8 (over z_hi, core).
Axes of the slice: x: 4, y: 8, z: 8 (z_hi: 4, z_lo: 2; z = z_hi * 2 + z_lo), core: 2. Of those that a mesh axis runs over, the one named last changes fastest.
Arguments:
- queries: bfloat16 [8192, 4096], P(('ctx', 'head')), may hold values from -30 to 30
- keys: bfloat16 [8192, 1024], P(('ctx', 'head')), may hold values from -6 to 6
- values: bfloat16 [8192, 1024], P(('ctx', 'head')), may hold values from -6 to 6
- outputs: bfloat16 [8192, 4096], P(('ctx', 'head')), may hold values from -6 to 6
- output_gradient: bfloat16 [8192, 4096], P(('ctx', 'head')), may hold values from -6 to 6
- importance: int32 [8192], P('ctx'), may hold values from 0 to 8
- span_order: int32 [128], replicated, may hold values from 0 to 127, each once
Outputs:
- query_grad: bfloat16 [8192, 4096], P(('ctx', 'head'))
- key_gradient: bfloat16 [8192, 1024], P(('ctx', 'head'))
- value_gradient: bfloat16 [8192, 1024], P(('ctx', 'head'))
The draws below stay inside these ranges and needn't reach their ends.
All inputs are finite; a program needn't handle non-finite values.
Results may differ from the reference program's by a relative error of at most 0.0049.
Values may be sent and summed in bfloat16 or wider, within the bound.
A program may use at most 64 MiB of HBM per device.

```python
import math
import jax
import jax.numpy as jnp
from jax import lax

QUERY_HEADS = 32
KEY_VALUE_HEADS = 8
HEAD_WIDTH = 128
CH = 64
NCHUNK = 128
TOKEN_COUNT = 8192


def shared_draw(key):
    query_draw = jax.random.fold_in(key, 101)
    random_keys = jax.random.fold_in(key, 102)
    query_base = jnp.clip(jax.random.normal(query_draw, (TOKEN_COUNT, QUERY_HEADS * HEAD_WIDTH), jnp.float32), -6.0, 6.0)
    key_start = jnp.clip(jax.random.normal(random_keys, (TOKEN_COUNT, KEY_VALUE_HEADS * HEAD_WIDTH), jnp.float32), -6.0, 6.0)
    return (query_base, key_start)


def draw_queries(key, part):
    return shared_draw(key)[0].astype(jnp.bfloat16)


def draw_keys(key, part):
    return shared_draw(key)[1].astype(jnp.bfloat16)


def touch_ends(result, key, smallest, top_value):
    spot = [jax.random.randint(jax.random.fold_in(key, axis), (), 0, length) for axis, length in enumerate(result.shape)]
    main_axis = result.shape.index(max(result.shape))
    next_to = spot[:main_axis] + [(spot[main_axis] + 1) % result.shape[main_axis]] + spot[main_axis + 1:]
    return result.at[tuple(spot)].set(smallest).at[tuple(next_to)].set(top_value)


def steps_of(own_key, shape, shards, smallest, largest):
    loudness, own = 1.0, jax.random.fold_in(own_key, 6)
    for axis_at, blocks in shards:
        draws = jnp.exp(jax.random.uniform(jax.random.fold_in(own, axis_at), (blocks,), jnp.float32, smallest / len(shards), largest / len(shards)))
        loudness = loudness * jnp.repeat(draws, shape[axis_at] // blocks).reshape([-1 if axis == axis_at else 1 for axis in range(len(shape))])
    return loudness


def normal_values(rng, shape, scale, most, pieces=(), held_as=jnp.bfloat16):
    result = scale * jax.random.normal(rng, shape, jnp.float32)
    if pieces:
        result = result * steps_of(rng, shape, pieces, -0.22, 0.18)
    return jnp.clip(result, -most, most).astype(held_as)


def setup_inputs(seed: int = 0) -> dict:
    arg_keys = jax.random.split(jax.random.key(seed), 8)
    queries = draw_queries(jax.random.fold_in(arg_keys[7], 71), 0)
    keys = draw_keys(jax.random.fold_in(arg_keys[7], 71), 0)
    values = normal_values(arg_keys[2], (TOKEN_COUNT, KEY_VALUE_HEADS * HEAD_WIDTH), 1.0, 6.0, ((0, 512),))
    outputs = normal_values(arg_keys[3], (TOKEN_COUNT, QUERY_HEADS * HEAD_WIDTH), 1.0, 6.0, ((0, 512),))
    output_gradient = normal_values(arg_keys[4], (TOKEN_COUNT, QUERY_HEADS * HEAD_WIDTH), 1.0, 6.0, ((0, 512),))
    importance = touch_ends(jax.random.randint(arg_keys[5], (TOKEN_COUNT,), 0, 9), jax.random.fold_in(arg_keys[5], 1), 0, 8).astype(jnp.int32)
    span_order = jax.random.permutation(arg_keys[6], NCHUNK).astype(jnp.int32)
    return dict(queries=queries, keys=keys, values=values, outputs=outputs, output_gradient=output_gradient, importance=importance, span_order=span_order)


def reference(queries, keys, values, outputs, output_gradient, importance, span_order):
    token_index = jnp.arange(TOKEN_COUNT, dtype=jnp.int32)
    positions = span_order[token_index // CH] * CH + token_index % CH
    visible = positions[None, :] <= positions[:, None]
    token_gain = importance.astype(jnp.float32) * 0.25
    score_scale = 1.0 / math.sqrt(HEAD_WIDTH)
    group_width = QUERY_HEADS // KEY_VALUE_HEADS
    heads_of_queries = queries.reshape(TOKEN_COUNT, KEY_VALUE_HEADS, group_width, HEAD_WIDTH).transpose(1, 2, 0, 3)
    gradient_heads = output_gradient.reshape(TOKEN_COUNT, KEY_VALUE_HEADS, group_width, HEAD_WIDTH).transpose(1, 2, 0, 3)
    heads_of_output = outputs.reshape(TOKEN_COUNT, KEY_VALUE_HEADS, group_width, HEAD_WIDTH).transpose(1, 2, 0, 3)
    heads_of_keys = keys.reshape(TOKEN_COUNT, KEY_VALUE_HEADS, HEAD_WIDTH).transpose(1, 0, 2)
    heads_of_values = values.reshape(TOKEN_COUNT, KEY_VALUE_HEADS, HEAD_WIDTH).transpose(1, 0, 2)

    def one_group(inputs):
        key_block, value_block, query_group, grad_group, out_group = inputs

        def one_head(running_sums, head_inputs):
            query_one, grad_one, out_one = head_inputs
            raw_scores = jnp.dot(query_one, key_block.T, preferred_element_type=jnp.float32) * score_scale
            masked = jnp.where(visible, raw_scores, -jnp.inf)
            row_max = lax.optimization_barrier(jnp.max(masked, axis=1))
            log_norm = row_max + jnp.log(lax.optimization_barrier(jnp.sum(jnp.exp(masked - row_max[:, None]), axis=1)))
            probs = jnp.where(visible, jnp.exp(raw_scores - log_norm[:, None]), 0.0)
            prob_grads = jnp.dot(grad_one, value_block.T, preferred_element_type=jnp.float32)
            out_dot = lax.optimization_barrier(jnp.sum(grad_one.astype(jnp.float32) * out_one.astype(jnp.float32), axis=1))
            score_grads = (probs * (prob_grads - out_dot[:, None]) * (token_gain * score_scale)[:, None]).astype(jnp.bfloat16)
            weighted = (probs * token_gain[:, None]).astype(jnp.bfloat16)
            query_part = jnp.dot(score_grads, key_block, preferred_element_type=jnp.float32).astype(jnp.bfloat16)
            key_sum = running_sums[0] + jnp.dot(score_grads.T, query_one, preferred_element_type=jnp.float32)
            value_sum = running_sums[1] + jnp.dot(weighted.T, grad_one, preferred_element_type=jnp.float32)
            return ((key_sum, value_sum), query_part)
        start_sums = (jnp.zeros((TOKEN_COUNT, HEAD_WIDTH), jnp.float32), jnp.zeros((TOKEN_COUNT, HEAD_WIDTH), jnp.float32))
        final_sums, query_parts = lax.scan(one_head, start_sums, (query_group, grad_group, out_group))
        return (query_parts, final_sums[0].astype(jnp.bfloat16), final_sums[1].astype(jnp.bfloat16))
    query_parts, key_pieces, value_pieces = lax.map(one_group, (heads_of_keys, heads_of_values, heads_of_queries, gradient_heads, heads_of_output))
    query_grad = query_parts.transpose(2, 0, 1, 3).reshape(TOKEN_COUNT, QUERY_HEADS * HEAD_WIDTH)
    key_gradient = key_pieces.transpose(1, 0, 2).reshape(TOKEN_COUNT, KEY_VALUE_HEADS * HEAD_WIDTH)
    value_gradient = value_pieces.transpose(1, 0, 2).reshape(TOKEN_COUNT, KEY_VALUE_HEADS * HEAD_WIDTH)
    return (query_grad, key_gradient, value_gradient)
```

```python
import functools
import math

import jax
import jax.numpy as jnp
from jax import lax
from jax.experimental import pallas as pl
from jax.experimental.pallas import tpu as pltpu
from jax.sharding import PartitionSpec as P

QUERY_HEADS = 32
KEY_VALUE_HEADS = 8
GROUP = 4
WIDTH = 128
CH = 64
HEADS = 8
NX = 4
NJ = 16
OWN = 16
BLOCK = 128
QT = NX * BLOCK
KT = NJ * BLOCK
KB = 512
SCALE = 1.0 / math.sqrt(WIDTH)
SCALE2 = SCALE * math.log2(math.e)
LOW = -1e30
FLOOR = -1e20

MESH = pl.DeviceIdType.MESH
VMEM = pl.BlockSpec(memory_space=pltpu.VMEM)
SMEM = pl.BlockSpec(memory_space=pltpu.SMEM)
NT = (((1,), (1,)), ((), ()))
TN = (((0,), (0,)), ((), ()))


def place():
    ctx = lax.axis_index("ctx")
    return ctx // NJ, lax.rem(ctx, NJ), lax.axis_index("head")


def head_peer(i, j, h, d):
    return {"ctx": i * NJ + j, "head": lax.rem(h + d, HEADS)}


def x_peer(i, j, h, d):
    return {"ctx": lax.rem(i + d, NX) * NJ + j, "head": h}


def j_peer(i, j, h, d):
    return {"ctx": i * NJ + lax.rem(j + d, NJ), "head": h}


def greet(peers):
    barrier = pltpu.get_barrier_semaphore()
    for peer in peers:
        pl.semaphore_signal(barrier, inc=1, device_id=peer, device_id_type=MESH)
    pl.semaphore_wait(barrier, len(peers))


def remote(src, dst, send, recv, peer):
    return pltpu.make_async_remote_copy(
        src_ref=src, dst_ref=dst, send_sem=send, recv_sem=recv, device_id=peer, device_id_type=MESH
    )


def cols(index, width):
    return pl.ds(pl.multiple_of(index * width, width), width)


def gather_kernel(
    q_ref, g_ref, k_ref, v_ref, e_ref, qa, ga, ka, va, ea,
    local_sem, send1, recv1, send2, recv2, send3, recv3,
):
    i, j, h = place()
    greet(
        [head_peer(i, j, h, d) for d in range(1, HEADS)]
        + [x_peer(i, j, h, d) for d in range(1, NX)]
        + [j_peer(i, j, h, d) for d in range(1, NJ)]
    )

    def pieces(c):
        mine_q = cols(i * HEADS + h, OWN)
        mine_k = cols(j * HEADS + h, OWN)
        mine_e = cols(i * HEADS + h, 8)
        return [
            (k_ref.at[:, cols(c, WIDTH)], ka.at[mine_k, :]),
            (v_ref.at[:, cols(c, WIDTH)], va.at[mine_k, :]),
            (q_ref.at[:, cols(c, GROUP * WIDTH)], qa.at[mine_q, :]),
            (g_ref.at[:, cols(c, GROUP * WIDTH)], ga.at[mine_q, :]),
            (e_ref.at[cols(c, 8), :], ea.at[mine_e, :]),
        ]

    first = []
    for d in range(1, HEADS):
        for n, (src, dst) in enumerate(pieces(lax.rem(h + d, HEADS))):
            copy = remote(src, dst, send1.at[d, n], recv1.at[d, n], head_peer(i, j, h, d))
            copy.start()
            first.append((n, copy))
    own = []
    for n, (src, dst) in enumerate(pieces(h)):
        copy = pltpu.make_async_copy(src, dst, local_sem.at[n])
        copy.start()
        own.append((n, copy))
    for n, copy in own:
        copy.wait()
    for n, copy in first:
        if n < 2:
            copy.wait_recv()
    second = []
    for d in range(1, NJ):
        rows = cols(j, BLOCK)
        for n, ref in enumerate((ka, va)):
            copy = remote(
                ref.at[rows, :], ref.at[rows, :], send3.at[d, n], recv3.at[d, n], j_peer(i, j, h, d)
            )
            copy.start()
            second.append(copy)
    for n, copy in first:
        if n >= 2:
            copy.wait_recv()
    for d in range(1, NX):
        rows = cols(i, BLOCK)
        erows = cols(i, HEADS * 8)
        for n, (ref, part) in enumerate(((qa, rows), (ga, rows), (ea, erows))):
            copy = remote(
                ref.at[part, :], ref.at[part, :], send2.at[d, n], recv2.at[d, n], x_peer(i, j, h, d)
            )
            copy.start()
            second.append(copy)
    for copy in second:
        copy.wait_recv()
    for n, copy in first:
        copy.wait_send()
    for copy in second:
        copy.wait_send()


def gather(queries, grads, keys, values, extra):
    shapes = (
        jax.ShapeDtypeStruct((QT, GROUP * WIDTH), jnp.bfloat16),
        jax.ShapeDtypeStruct((QT, GROUP * WIDTH), jnp.bfloat16),
        jax.ShapeDtypeStruct((KT, WIDTH), jnp.bfloat16),
        jax.ShapeDtypeStruct((KT, WIDTH), jnp.bfloat16),
        jax.ShapeDtypeStruct((NX * HEADS * 8, 128), jnp.float32),
    )
    dma = pltpu.SemaphoreType.DMA
    return pl.pallas_call(
        gather_kernel,
        out_shape=shapes,
        in_specs=[VMEM] * 5,
        out_specs=[VMEM] * 5,
        scratch_shapes=[
            dma((5,)),
            dma((HEADS, 5)),
            dma((HEADS, 5)),
            dma((NX, 3)),
            dma((NX, 3)),
            dma((NJ, 2)),
            dma((NJ, 2)),
        ],
        compiler_params=pltpu.CompilerParams(collective_id=0, has_side_effects=True),
        name="gather",
    )(queries, grads, keys, values, extra)


def masked_scores(spans, start, qpos, key_block, query_head):
    scores = lax.dot_general(key_block, query_head, NT, preferred_element_type=jnp.float32)
    row = lax.broadcasted_iota(jnp.int32, (CH, QT), 0) - qpos
    count = key_block.shape[0] // CH
    parts = [
        jnp.where(row <= -CH * spans[start + n], scores[n * CH : (n + 1) * CH], LOW)
        for n in range(count)
    ]
    return jnp.concatenate(parts, axis=0)


def stats_kernel(spans, qpos_ref, q_ref, k_ref, out_ref):
    qpos = qpos_ref[...]

    def step(b, carry):
        key_block = k_ref[pl.ds(pl.multiple_of(b * KB, KB), KB), :]
        following = []
        for g in range(GROUP):
            top, total = carry[g]
            scores = masked_scores(
                spans, b * (KB // CH), qpos, key_block, q_ref[:, g * WIDTH : (g + 1) * WIDTH]
            )
            new_top = jnp.maximum(top, jnp.max(scores, axis=0, keepdims=True))
            total = total * jnp.exp2((top - new_top) * SCALE2) + jnp.sum(
                jnp.exp2((scores - new_top) * SCALE2), axis=0, keepdims=True
            )
            following.append((new_top, total))
        return tuple(following)

    start = tuple(
        (jnp.full((1, QT), FLOOR, jnp.float32), jnp.zeros((1, QT), jnp.float32))
        for g in range(GROUP)
    )
    result = lax.fori_loop(0, KT // KB, step, start)
    for g in range(GROUP):
        out_ref[g : g + 1, :] = result[g][0]
        out_ref[GROUP + g : GROUP + g + 1, :] = result[g][1]


def stats(spans, qpos, queries, keys):
    return pl.pallas_call(
        stats_kernel,
        out_shape=jax.ShapeDtypeStruct((2 * GROUP, QT), jnp.float32),
        in_specs=[SMEM, VMEM, VMEM, VMEM],
        out_specs=VMEM,
        name="stats",
    )(spans, qpos, queries, keys)


def share_kernel(in_ref, out_ref, local_sem, send, recv):
    i, j, h = place()
    greet([x_peer(i, j, h, d) for d in range(1, NX)])
    mine = out_ref.at[cols(i, 2 * GROUP), :]
    copies = []
    for d in range(1, NX):
        copy = remote(in_ref, mine, send.at[d], recv.at[d], x_peer(i, j, h, d))
        copy.start()
        copies.append(copy)
    own = pltpu.make_async_copy(in_ref, mine, local_sem)
    own.start()
    own.wait()
    for copy in copies:
        copy.wait_recv()
    for copy in copies:
        copy.wait_send()


def share(values):
    dma = pltpu.SemaphoreType.DMA
    return pl.pallas_call(
        share_kernel,
        out_shape=jax.ShapeDtypeStruct((NX * 2 * GROUP, QT), jnp.float32),
        in_specs=[VMEM],
        out_specs=VMEM,
        scratch_shapes=[dma, dma((NX,)), dma((NX,))],
        compiler_params=pltpu.CompilerParams(collective_id=1, has_side_effects=True),
        name="share",
    )(values)


def grads_kernel(
    spans, qpos_ref, stats_ref, extra_ref, q_ref, g_ref, k_ref, v_ref, dq_ref, dk_ref, dv_ref, acc
):
    qpos = qpos_ref[...]
    gain = extra_ref[GROUP : GROUP + 1, :]
    gain_scale = gain * SCALE
    norms = []
    for g in range(GROUP):
        tops = [stats_ref[x * 2 * GROUP + g :][:1, :] for x in range(NX)]
        totals = [stats_ref[x * 2 * GROUP + GROUP + g :][:1, :] for x in range(NX)]
        top = functools.reduce(jnp.maximum, tops)
        total = sum(t * jnp.exp2((m - top) * SCALE2) for m, t in zip(tops, totals))
        norms.append(top * SCALE2 + jnp.log2(total))
    acc[...] = jnp.zeros_like(acc)

    def step(b, carry):
        rows = pl.ds(pl.multiple_of(b * KB, KB), KB)
        key_block = k_ref[rows, :]
        value_block = v_ref[rows, :]
        key_grad = jnp.zeros((KB, WIDTH), jnp.float32)
        value_grad = jnp.zeros((KB, WIDTH), jnp.float32)
        for g in range(GROUP):
            part = slice(g * WIDTH, (g + 1) * WIDTH)
            query_head = q_ref[:, part]
            grad_head = g_ref[:, part]
            scores = masked_scores(spans, b * (KB // CH), qpos, key_block, query_head)
            probs = jnp.exp2(scores * SCALE2 - norms[g])
            prob_grads = lax.dot_general(
                value_block, grad_head, NT, preferred_element_type=jnp.float32
            )
            out_dot = extra_ref[g : g + 1, :]
            weighted = (probs * gain).astype(jnp.bfloat16)
            score_grads = (probs * ((prob_grads - out_dot) * gain_scale)).astype(jnp.bfloat16)
            key_grad += jnp.dot(score_grads, query_head, preferred_element_type=jnp.float32)
            value_grad += jnp.dot(weighted, grad_head, preferred_element_type=jnp.float32)
            acc[:, part] += lax.dot_general(
                score_grads, key_block, TN, preferred_element_type=jnp.float32
            )
        dk_ref[rows, :] = key_grad.astype(jnp.bfloat16)
        dv_ref[rows, :] = value_grad.astype(jnp.bfloat16)
        return carry

    lax.fori_loop(0, KT // KB, step, 0)
    dq_ref[...] = acc[...].astype(jnp.bfloat16)


def grads(spans, qpos, all_stats, extra, queries, out_grads, keys, values):
    return pl.pallas_call(
        grads_kernel,
        out_shape=(
            jax.ShapeDtypeStruct((QT, GROUP * WIDTH), jnp.bfloat16),
            jax.ShapeDtypeStruct((KT, WIDTH), jnp.bfloat16),
            jax.ShapeDtypeStruct((KT, WIDTH), jnp.bfloat16),
        ),
        in_specs=[SMEM] + [VMEM] * 7,
        out_specs=[VMEM] * 3,
        scratch_shapes=[pltpu.VMEM((QT, GROUP * WIDTH), jnp.float32)],
        name="grads",
    )(spans, qpos, all_stats, extra, queries, out_grads, keys, values)


def scatter_kernel(
    dq_ref, dk_ref, dv_ref, oq, ok, ov, rq, rk, rv, sq, sk, sv,
    local_sem, send1, recv1, send2, recv2, send3, recv3,
):
    i, j, h = place()
    greet(
        [head_peer(i, j, h, d) for d in range(1, HEADS)]
        + [x_peer(i, j, h, d) for d in range(1, NX)]
        + [j_peer(i, j, h, d) for d in range(1, NJ)]
    )
    pairs = []
    for d in range(1, NJ):
        rows = cols(lax.rem(j + d, NJ), BLOCK)
        for n, (src, dst) in enumerate(((dk_ref, rk), (dv_ref, rv))):
            copy = remote(
                src.at[rows, :], dst.at[d - 1], send3.at[d, n], recv3.at[d, n], j_peer(i, j, h, d)
            )
            copy.start()
            pairs.append(copy)
    query_parts = []
    for d in range(1, NX):
        rows = cols(lax.rem(i + d, NX), BLOCK)
        copy = remote(dq_ref.at[rows, :], rq.at[d - 1], send1.at[d], recv1.at[d], x_peer(i, j, h, d))
        copy.start()
        query_parts.append(copy)
    for copy in query_parts:
        copy.wait_recv()
    total = dq_ref[cols(i, BLOCK), :].astype(jnp.float32)
    for d in range(1, NX):
        total += rq[d - 1].astype(jnp.float32)
    sq[...] = total.astype(jnp.bfloat16)
    for copy in pairs:
        copy.wait_recv()
    for src, dst, out in ((dk_ref, rk, sk), (dv_ref, rv, sv)):
        total = src[cols(j, BLOCK), :].astype(jnp.float32)
        for d in range(1, NJ):
            total += dst[d - 1].astype(jnp.float32)
        out[...] = total.astype(jnp.bfloat16)

    def pieces(c):
        rows = cols(c, OWN)
        return [
            (sq.at[rows, :], oq.at[:, cols(h, GROUP * WIDTH)]),
            (sk.at[rows, :], ok.at[:, cols(h, WIDTH)]),
            (sv.at[rows, :], ov.at[:, cols(h, WIDTH)]),
        ]

    last = []
    for d in range(1, HEADS):
        for n, (src, dst) in enumerate(pieces(lax.rem(h + d, HEADS))):
            copy = remote(src, dst, send2.at[d, n], recv2.at[d, n], head_peer(i, j, h, d))
            copy.start()
            last.append(copy)
    own = []
    for n, (src, dst) in enumerate(pieces(h)):
        copy = pltpu.make_async_copy(src, dst, local_sem.at[n])
        copy.start()
        own.append(copy)
    for copy in own:
        copy.wait()
    for copy in last:
        copy.wait_recv()
    for copy in pairs + query_parts + last:
        copy.wait_send()


def scatter(dq, dk, dv):
    dma = pltpu.SemaphoreType.DMA
    bf16 = jnp.bfloat16
    return pl.pallas_call(
        scatter_kernel,
        out_shape=(
            jax.ShapeDtypeStruct((OWN, QUERY_HEADS * WIDTH), bf16),
            jax.ShapeDtypeStruct((OWN, KEY_VALUE_HEADS * WIDTH), bf16),
            jax.ShapeDtypeStruct((OWN, KEY_VALUE_HEADS * WIDTH), bf16),
        ),
        in_specs=[VMEM] * 3,
        out_specs=[VMEM] * 3,
        scratch_shapes=[
            pltpu.VMEM((NX - 1, BLOCK, GROUP * WIDTH), bf16),
            pltpu.VMEM((NJ - 1, BLOCK, WIDTH), bf16),
            pltpu.VMEM((NJ - 1, BLOCK, WIDTH), bf16),
            pltpu.VMEM((BLOCK, GROUP * WIDTH), bf16),
            pltpu.VMEM((BLOCK, WIDTH), bf16),
            pltpu.VMEM((BLOCK, WIDTH), bf16),
            dma((3,)),
            dma((NX,)),
            dma((NX,)),
            dma((HEADS, 3)),
            dma((HEADS, 3)),
            dma((NJ, 2)),
            dma((NJ, 2)),
        ],
        compiler_params=pltpu.CompilerParams(collective_id=2, has_side_effects=True),
        name="scatter",
    )(dq, dk, dv)


def on_device(queries, keys, values, outputs, output_gradient, importance, span_order):
    i, j, h = place()
    out_dot = jnp.sum(
        (output_gradient.astype(jnp.float32) * outputs.astype(jnp.float32)).reshape(
            OWN, KEY_VALUE_HEADS, GROUP, WIDTH
        ),
        axis=-1,
    ).transpose(1, 2, 0)
    own_gain = lax.dynamic_slice_in_dim(importance.astype(jnp.float32) * 0.25, h * OWN, OWN)
    extra = jnp.concatenate(
        [out_dot, jnp.broadcast_to(own_gain, (KEY_VALUE_HEADS, 1, OWN))], axis=1
    )
    extra = jnp.pad(extra, ((0, 0), (0, 8 - GROUP - 1), (0, 128 - OWN)))
    qa, ga, ka, va, ea = gather(
        queries, output_gradient, keys, values, extra.reshape(KEY_VALUE_HEADS * 8, 128)
    )
    extra_all = ea.reshape(NX, HEADS, 8, 128)[..., :OWN].transpose(2, 0, 1, 3).reshape(8, QT)
    query_spans = lax.dynamic_index_in_dim(span_order.reshape(NX, NJ, 2), j, 1, keepdims=False)
    qpos = (query_spans.reshape(-1, 1) * CH + jnp.arange(CH, dtype=jnp.int32)).reshape(1, QT)
    spans = lax.dynamic_slice_in_dim(span_order, i * (KT // CH), KT // CH)
    own_stats = stats(spans, qpos, qa, ka)
    all_stats = share(own_stats)
    dq, dk, dv = grads(spans, qpos, all_stats, extra_all, qa, ga, ka, va)
    return scatter(dq, dk, dv)


def solution(mesh):
    tokens = P(("ctx", "head"), None)
    return jax.shard_map(
        on_device,
        mesh=mesh,
        in_specs=(tokens, tokens, tokens, tokens, tokens, P("ctx"), P()),
        out_specs=(tokens, tokens, tokens),
        check_vma=False,
    )
```

```python
import functools
import math

import jax
import jax.numpy as jnp
from jax import lax
from jax.experimental import pallas as pl
from jax.experimental.pallas import tpu as pltpu
from jax.sharding import PartitionSpec as P

QUERY_HEADS = 32
KEY_VALUE_HEADS = 8
GROUP = 4
WIDTH = 128
CH = 64
HEADS = 8
NX = 4
NJ = 16
NY = 8
OWN = 16
BLOCK = 128
QT = NX * BLOCK
KT = NJ * BLOCK
KB = 512
SCALE = 1.0 / math.sqrt(WIDTH)
SCALE2 = SCALE * math.log2(math.e)
LOW = -1e30
FLOOR = -1e20

MESH = pl.DeviceIdType.MESH
VMEM = pl.BlockSpec(memory_space=pltpu.VMEM)
SMEM = pl.BlockSpec(memory_space=pltpu.SMEM)
NT = (((1,), (1,)), ((), ()))
TN = (((0,), (0,)), ((), ()))


def place():
    ctx = lax.axis_index("ctx")
    return ctx // NJ, lax.rem(ctx, NJ), lax.axis_index("head")


def head_peer(i, j, h, d):
    return {"ctx": i * NJ + j, "head": lax.rem(h + d, HEADS)}


def x_peer(i, j, h, d):
    return {"ctx": lax.rem(i + d, NX) * NJ + j, "head": h}


def greet(peers):
    barrier = pltpu.get_barrier_semaphore()
    for peer in peers:
        pl.semaphore_signal(barrier, inc=1, device_id=peer, device_id_type=MESH)
    pl.semaphore_wait(barrier, len(peers))


def remote(src, dst, send, recv, peer):
    return pltpu.make_async_remote_copy(
        src_ref=src, dst_ref=dst, send_sem=send, recv_sem=recv, device_id=peer, device_id_type=MESH
    )


def cols(index, width):
    return pl.ds(pl.multiple_of(index * width, width), width)


def z_peer(i, j, h):
    return {"ctx": i * NJ + lax.rem(j + NY, NJ), "head": h}


def y_peer(i, j, h, d):
    return {"ctx": i * NJ + (j // NY) * NY + lax.rem(lax.rem(j, NY) + d + NY, NY), "head": h}


def ring_block(j, zc, d):
    other = lax.rem(j // NY + zc, 2)
    return other * NY + lax.rem(lax.rem(j, NY) + d + 2 * NY, NY)


def all_peers(i, j, h):
    return (
        [head_peer(i, j, h, d) for d in range(1, HEADS)]
        + [x_peer(i, j, h, d) for d in range(1, NX)]
        + [z_peer(i, j, h), y_peer(i, j, h, 1), y_peer(i, j, h, -1)]
    )


def gather_kernel(
    q_ref, g_ref, k_ref, v_ref, e_ref, qa, ga, ka, va, ea, ep,
    local_sem, send1, recv1, send2, recv2, send3, recv3, send4, recv4, send5, recv5,
):
    i, j, h = place()
    greet(all_peers(i, j, h))

    def pieces(c):
        mine_q = cols(i * HEADS + h, OWN)
        mine_k = cols(j * HEADS + h, OWN)
        return [
            (k_ref.at[:, cols(c, WIDTH)], ka.at[mine_k, :]),
            (v_ref.at[:, cols(c, WIDTH)], va.at[mine_k, :]),
            (q_ref.at[:, cols(c, GROUP * WIDTH)], qa.at[mine_q, :]),
            (g_ref.at[:, cols(c, GROUP * WIDTH)], ga.at[mine_q, :]),
            (e_ref.at[cols(c, 8), :], ep.at[cols(h, 8), :]),
        ]

    first = []
    for n in range(5):
        for d in range(1, HEADS):
            src, dst = pieces(lax.rem(h + d, HEADS))[n]
            copy = remote(src, dst, send1.at[d, n], recv1.at[d, n], head_peer(i, j, h, d))
            copy.start()
            first.append((n, copy))
    own = []
    for n, (src, dst) in enumerate(pieces(h)):
        copy = pltpu.make_async_copy(src, dst, local_sem.at[n])
        copy.start()
        own.append(copy)
    for copy in own:
        copy.wait()
    for n, copy in first:
        if n < 2:
            copy.wait_recv()
    sent = []

    def push(ref, rows, send, recv, peer):
        copy = remote(ref.at[rows, :], ref.at[rows, :], send, recv, peer)
        copy.start()
        sent.append(copy)
        return copy

    pair = (ka, va)
    ways = (1, -1)
    ring = {}

    def ring_push(step, zc, way, kinds):
        rows = cols(ring_block(j, zc, -ways[way] * (step - 1)), BLOCK)
        for n in kinds:
            at = (way, step - 1, zc, n)
            ring[way, step, zc, n] = push(
                pair[n], rows, send3.at[at], recv3.at[at], y_peer(i, j, h, ways[way])
            )

    across = [
        push(pair[n], cols(j, BLOCK), send4.at[n], recv4.at[n], z_peer(i, j, h)) for n in range(2)
    ]
    for way in range(2):
        ring_push(1, 0, way, (0, 1))
    for n, copy in first:
        if n >= 2:
            copy.wait_recv()
    x_rows = cols(i, BLOCK)
    x_first = [
        [
            push(ref, x_rows, send2.at[way, 0, n], recv2.at[way, 0, n], x_peer(i, j, h, d))
            for n, ref in enumerate((qa, ga))
        ]
        for way, d in enumerate((1, NX - 1))
    ]
    for copy in across:
        copy.wait_recv()
    for way in range(2):
        ring_push(1, 1, way, (0, 1))
    ea[cols(i, 8), :] = jnp.concatenate(
        [ep[8 * n : 8 * n + 8, :OWN] for n in range(HEADS)], axis=1
    )
    extras = [
        push(ea, cols(i, 8), send5.at[d], recv5.at[d], x_peer(i, j, h, d)) for d in range(1, NX)
    ]
    for step in range(2, 5):
        for zc in range(2):
            for way in range(2):
                for n in range(2):
                    ring[way, step - 1, zc, n].wait_recv()
                ring_push(step, zc, way, (0, 1) if step < 4 else (way,))
        if step == 3:
            for copies in x_first:
                for copy in copies:
                    copy.wait_recv()
            x_last = []
            for way, (ref, d) in enumerate(((qa, 1), (ga, NX - 1))):
                rows = cols(lax.rem(i - (1, -1)[way] + NX, NX), BLOCK)
                x_last.append(
                    push(ref, rows, send2.at[way, 1, 0], recv2.at[way, 1, 0], x_peer(i, j, h, d))
                )
    for zc in range(2):
        for way in range(2):
            ring[way, 4, zc, way].wait_recv()
    for copy in x_last + extras:
        copy.wait_recv()
    for n, copy in first:
        copy.wait_send()
    for copy in sent:
        copy.wait_send()


def gather(queries, grads, keys, values, extra):
    shapes = (
        jax.ShapeDtypeStruct((QT, GROUP * WIDTH), jnp.bfloat16),
        jax.ShapeDtypeStruct((QT, GROUP * WIDTH), jnp.bfloat16),
        jax.ShapeDtypeStruct((KT, WIDTH), jnp.bfloat16),
        jax.ShapeDtypeStruct((KT, WIDTH), jnp.bfloat16),
        jax.ShapeDtypeStruct((NX * 8, 128), jnp.float32),
    )
    dma = pltpu.SemaphoreType.DMA
    return pl.pallas_call(
        gather_kernel,
        out_shape=shapes,
        in_specs=[VMEM] * 5,
        out_specs=[VMEM] * 5,
        scratch_shapes=[
            pltpu.VMEM((HEADS * 8, 128), jnp.float32),
            dma((5,)),
            dma((HEADS, 5)),
            dma((HEADS, 5)),
            dma((2, 2, 2)),
            dma((2, 2, 2)),
            dma((2, 4, 2, 2)),
            dma((2, 4, 2, 2)),
            dma((2,)),
            dma((2,)),
            dma((NX,)),
            dma((NX,)),
        ],
        compiler_params=pltpu.CompilerParams(collective_id=0, has_side_effects=True),
        name="gather",
    )(queries, grads, keys, values, extra)


def query_positions(spans):
    i, j, h = place()
    lane = lax.broadcasted_iota(jnp.int32, (1, BLOCK), 1)
    rows = []
    for x in range(NX):
        at = 2 * (x * NJ + j)
        start = jnp.where(lane < CH, spans[at] * CH, spans[at + 1] * CH - CH)
        rows.append(start + lane)
    return jnp.concatenate(rows, axis=1)


def extra_row(extra_ref, n):
    return jnp.concatenate([extra_ref[8 * x + n : 8 * x + n + 1, :] for x in range(NX)], axis=1)


def masked_scores(spans, start, qpos, key_block, query_head):
    scores = lax.dot_general(key_block, query_head, NT, preferred_element_type=jnp.float32)
    row = lax.broadcasted_iota(jnp.int32, (CH, QT), 0) - qpos
    count = key_block.shape[0] // CH
    parts = [
        jnp.where(row <= -CH * spans[start + n], scores[n * CH : (n + 1) * CH], LOW)
        for n in range(count)
    ]
    return jnp.concatenate(parts, axis=0)


def stats_kernel(spans, q_ref, k_ref, out_ref):
    qpos = query_positions(spans)
    first_span = (lax.axis_index("ctx") // NJ) * (KT // CH)

    def step(b, carry):
        key_block = k_ref[pl.ds(pl.multiple_of(b * KB, KB), KB), :]
        following = []
        for g in range(GROUP):
            top, total = carry[g]
            scores = masked_scores(
                spans, first_span + b * (KB // CH), qpos, key_block, q_ref[:, g * WIDTH : (g + 1) * WIDTH]
            )
            new_top = jnp.maximum(top, jnp.max(scores, axis=0, keepdims=True))
            total = total * jnp.exp2((top - new_top) * SCALE2) + jnp.sum(
                jnp.exp2((scores - new_top) * SCALE2), axis=0, keepdims=True
            )
            following.append((new_top, total))
        return tuple(following)

    start = tuple(
        (jnp.full((1, QT), FLOOR, jnp.float32), jnp.zeros((1, QT), jnp.float32))
        for g in range(GROUP)
    )
    result = lax.fori_loop(0, KT // KB, step, start)
    for g in range(GROUP):
        out_ref[g : g + 1, :] = result[g][0]
        out_ref[GROUP + g : GROUP + g + 1, :] = result[g][1]


def stats(spans, queries, keys):
    return pl.pallas_call(
        stats_kernel,
        out_shape=jax.ShapeDtypeStruct((2 * GROUP, QT), jnp.float32),
        in_specs=[SMEM, VMEM, VMEM],
        out_specs=VMEM,
        name="stats",
    )(spans, queries, keys)


def share_kernel(in_ref, out_ref, local_sem, send, recv):
    i, j, h = place()
    greet([x_peer(i, j, h, d) for d in range(1, NX)])
    mine = out_ref.at[cols(i, 2 * GROUP), :]
    copies = []
    for d in range(1, NX):
        copy = remote(in_ref, mine, send.at[d], recv.at[d], x_peer(i, j, h, d))
        copy.start()
        copies.append(copy)
    own = pltpu.make_async_copy(in_ref, mine, local_sem)
    own.start()
    own.wait()
    for copy in copies:
        copy.wait_recv()
    for copy in copies:
        copy.wait_send()


def share(values):
    dma = pltpu.SemaphoreType.DMA
    return pl.pallas_call(
        share_kernel,
        out_shape=jax.ShapeDtypeStruct((NX * 2 * GROUP, QT), jnp.float32),
        in_specs=[VMEM],
        out_specs=VMEM,
        scratch_shapes=[dma, dma((NX,)), dma((NX,))],
        compiler_params=pltpu.CompilerParams(collective_id=1, has_side_effects=True),
        name="share",
    )(values)


def grads_kernel(
    spans, stats_ref, extra_ref, q_ref, g_ref, k_ref, v_ref, dq_ref, dk_ref, dv_ref, acc
):
    qpos = query_positions(spans)
    first_span = (lax.axis_index("ctx") // NJ) * (KT // CH)
    gain = extra_row(extra_ref, GROUP)
    out_dots = [extra_row(extra_ref, g) for g in range(GROUP)]
    gain_scale = gain * SCALE
    norms = []
    for g in range(GROUP):
        tops = [stats_ref[x * 2 * GROUP + g :][:1, :] for x in range(NX)]
        totals = [stats_ref[x * 2 * GROUP + GROUP + g :][:1, :] for x in range(NX)]
        top = functools.reduce(jnp.maximum, tops)
        total = sum(t * jnp.exp2((m - top) * SCALE2) for m, t in zip(tops, totals))
        norms.append(top * SCALE2 + jnp.log2(total))
    acc[...] = jnp.zeros_like(acc)

    def step(b, carry):
        rows = pl.ds(pl.multiple_of(b * KB, KB), KB)
        key_block = k_ref[rows, :]
        value_block = v_ref[rows, :]
        key_grad = jnp.zeros((KB, WIDTH), jnp.float32)
        value_grad = jnp.zeros((KB, WIDTH), jnp.float32)
        for g in range(GROUP):
            part = slice(g * WIDTH, (g + 1) * WIDTH)
            query_head = q_ref[:, part]
            grad_head = g_ref[:, part]
            scores = masked_scores(spans, first_span + b * (KB // CH), qpos, key_block, query_head)
            probs = jnp.exp2(scores * SCALE2 - norms[g])
            prob_grads = lax.dot_general(
                value_block, grad_head, NT, preferred_element_type=jnp.float32
            )
            out_dot = out_dots[g]
            weighted = (probs * gain).astype(jnp.bfloat16)
            score_grads = (probs * ((prob_grads - out_dot) * gain_scale)).astype(jnp.bfloat16)
            key_grad += jnp.dot(score_grads, query_head, preferred_element_type=jnp.float32)
            value_grad += jnp.dot(weighted, grad_head, preferred_element_type=jnp.float32)
            acc[:, part] += lax.dot_general(
                score_grads, key_block, TN, preferred_element_type=jnp.float32
            )
        dk_ref[rows, :] = key_grad.astype(jnp.bfloat16)
        dv_ref[rows, :] = value_grad.astype(jnp.bfloat16)
        return carry

    lax.fori_loop(0, KT // KB, step, 0)
    dq_ref[...] = acc[...].astype(jnp.bfloat16)


def grads(spans, all_stats, extra, queries, out_grads, keys, values):
    return pl.pallas_call(
        grads_kernel,
        out_shape=(
            jax.ShapeDtypeStruct((QT, GROUP * WIDTH), jnp.bfloat16),
            jax.ShapeDtypeStruct((KT, WIDTH), jnp.bfloat16),
            jax.ShapeDtypeStruct((KT, WIDTH), jnp.bfloat16),
        ),
        in_specs=[SMEM] + [VMEM] * 6,
        out_specs=[VMEM] * 3,
        scratch_shapes=[pltpu.VMEM((QT, GROUP * WIDTH), jnp.float32)],
        name="grads",
    )(spans, all_stats, extra, queries, out_grads, keys, values)


def scatter_kernel(
    dq_ref, dk_ref, dv_ref, oq, ok, ov, rq, rr, run, zs, zr, sq, sk, sv,
    local_sem, send1, recv1, send2, recv2, send3, recv3, send4, recv4,
):
    i, j, h = place()
    greet(all_peers(i, j, h))
    sent = []

    def push(src, dst, send, recv, peer):
        copy = remote(src, dst, send, recv, peer)
        copy.start()
        sent.append(copy)
        return copy

    pair = (dk_ref, dv_ref)
    ways = (1, -1)
    ring = {}

    def ring_push(src, way, step, zc, n):
        at = (way, step - 1, zc, n)
        ring[way, step, zc, n] = push(
            src, rr.at[at], send3.at[at], recv3.at[at], y_peer(i, j, h, ways[way])
        )

    def target(way, step, zc):
        return cols(ring_block(j, zc, ways[way] * (5 - step)), BLOCK)

    for zc in (1, 0):
        for way in range(2):
            ring_push(pair[way].at[target(way, 1, zc), :], way, 1, zc, way)
    query_parts = []
    for d in range(1, NX):
        rows = cols(lax.rem(i + d, NX), BLOCK)
        query_parts.append(
            push(dq_ref.at[rows, :], rq.at[d - 1], send1.at[d], recv1.at[d], x_peer(i, j, h, d))
        )
    for zc in (1, 0):
        for way in range(2):
            ring_push(pair[1 - way].at[target(way, 2, zc), :], way, 2, zc, 1 - way)
    for step in range(2, 5):
        for zc in (1, 0):
            for way in range(2):
                for n in range(2) if step > 2 else (way,):
                    ring[way, step - 1, zc, n].wait_recv()
                    total = rr[way, step - 2, zc, n].astype(jnp.float32) + pair[n][
                        target(way, step, zc), :
                    ].astype(jnp.float32)
                    run[way, step - 2, zc, n] = total.astype(jnp.bfloat16)
                    ring_push(run.at[way, step - 2, zc, n], way, step, zc, n)
    for copy in query_parts:
        copy.wait_recv()
    total = dq_ref[cols(i, BLOCK), :].astype(jnp.float32)
    for d in range(1, NX):
        total += rq[d - 1].astype(jnp.float32)
    sq[...] = total.astype(jnp.bfloat16)

    def ring_total(zc, n):
        for way in range(2):
            ring[way, 4, zc, n].wait_recv()
        rows = cols(ring_block(j, zc, 0), BLOCK)
        return (
            pair[n][rows, :].astype(jnp.float32)
            + rr[0, 3, zc, n].astype(jnp.float32)
            + rr[1, 3, zc, n].astype(jnp.float32)
        )

    across = []
    for n in range(2):
        zs[n] = ring_total(1, n).astype(jnp.bfloat16)
        across.append(push(zs.at[n], zr.at[n], send4.at[n], recv4.at[n], z_peer(i, j, h)))
    for n, out in enumerate((sk, sv)):
        total = ring_total(0, n)
        across[n].wait_recv()
        out[...] = (total + zr[n].astype(jnp.float32)).astype(jnp.bfloat16)

    def pieces(c):
        rows = cols(c, OWN)
        return [
            (sq.at[rows, :], oq.at[:, cols(h, GROUP * WIDTH)]),
            (sk.at[rows, :], ok.at[:, cols(h, WIDTH)]),
            (sv.at[rows, :], ov.at[:, cols(h, WIDTH)]),
        ]

    last = []
    for d in range(1, HEADS):
        for n, (src, dst) in enumerate(pieces(lax.rem(h + d, HEADS))):
            last.append(push(src, dst, send2.at[d, n], recv2.at[d, n], head_peer(i, j, h, d)))
    own = []
    for n, (src, dst) in enumerate(pieces(h)):
        copy = pltpu.make_async_copy(src, dst, local_sem.at[n])
        copy.start()
        own.append(copy)
    for copy in own:
        copy.wait()
    for copy in last:
        copy.wait_recv()
    for copy in sent:
        copy.wait_send()


def scatter(dq, dk, dv):
    dma = pltpu.SemaphoreType.DMA
    bf16 = jnp.bfloat16
    return pl.pallas_call(
        scatter_kernel,
        out_shape=(
            jax.ShapeDtypeStruct((OWN, QUERY_HEADS * WIDTH), bf16),
            jax.ShapeDtypeStruct((OWN, KEY_VALUE_HEADS * WIDTH), bf16),
            jax.ShapeDtypeStruct((OWN, KEY_VALUE_HEADS * WIDTH), bf16),
        ),
        in_specs=[VMEM] * 3,
        out_specs=[VMEM] * 3,
        scratch_shapes=[
            pltpu.VMEM((NX - 1, BLOCK, GROUP * WIDTH), bf16),
            pltpu.VMEM((2, 4, 2, 2, BLOCK, WIDTH), bf16),
            pltpu.VMEM((2, 3, 2, 2, BLOCK, WIDTH), bf16),
            pltpu.VMEM((2, BLOCK, WIDTH), bf16),
            pltpu.VMEM((2, BLOCK, WIDTH), bf16),
            pltpu.VMEM((BLOCK, GROUP * WIDTH), bf16),
            pltpu.VMEM((BLOCK, WIDTH), bf16),
            pltpu.VMEM((BLOCK, WIDTH), bf16),
            dma((3,)),
            dma((NX,)),
            dma((NX,)),
            dma((HEADS, 3)),
            dma((HEADS, 3)),
            dma((2, 4, 2, 2)),
            dma((2, 4, 2, 2)),
            dma((2,)),
            dma((2,)),
        ],
        compiler_params=pltpu.CompilerParams(collective_id=2, has_side_effects=True),
        name="scatter",
    )(dq, dk, dv)


def on_device(queries, keys, values, outputs, output_gradient, importance, span_order):
    i, j, h = place()
    out_dot = jnp.sum(
        (output_gradient.astype(jnp.float32) * outputs.astype(jnp.float32)).reshape(
            OWN, KEY_VALUE_HEADS, GROUP, WIDTH
        ),
        axis=-1,
    ).transpose(1, 2, 0)
    own_gain = lax.dynamic_slice_in_dim(importance.astype(jnp.float32) * 0.25, h * OWN, OWN)
    extra = jnp.concatenate(
        [out_dot, jnp.broadcast_to(own_gain, (KEY_VALUE_HEADS, 1, OWN))], axis=1
    )
    extra = jnp.pad(extra, ((0, 0), (0, 8 - GROUP - 1), (0, 128 - OWN)))
    qa, ga, ka, va, ea = gather(
        queries, output_gradient, keys, values, extra.reshape(KEY_VALUE_HEADS * 8, 128)
    )
    own_stats = stats(span_order, qa, ka)
    all_stats = share(own_stats)
    dq, dk, dv = grads(span_order, all_stats, ea, qa, ga, ka, va)
    return scatter(dq, dk, dv)


def solution(mesh):
    tokens = P(("ctx", "head"), None)
    return jax.shard_map(
        on_device,
        mesh=mesh,
        in_specs=(tokens, tokens, tokens, tokens, tokens, P("ctx"), P()),
        out_specs=(tokens, tokens, tokens),
        check_vma=False,
    )
```

```python
import functools
import math

import jax
import jax.numpy as jnp
from jax import lax
from jax.experimental import pallas as pl
from jax.experimental.pallas import tpu as pltpu
from jax.sharding import PartitionSpec as P

QUERY_HEADS = 32
KEY_VALUE_HEADS = 8
GROUP = 4
WIDTH = 128
CH = 64
HEADS = 8
NX = 4
NJ = 16
NY = 8
OWN = 16
BLOCK = 128
QT = NX * BLOCK
KT = NJ * BLOCK
KB = 512
SCALE = 1.0 / math.sqrt(WIDTH)
SCALE2 = SCALE * math.log2(math.e)
LOW = -1e30
FLOOR = -1e20

MESH = pl.DeviceIdType.MESH
VMEM = pl.BlockSpec(memory_space=pltpu.VMEM)
SMEM = pl.BlockSpec(memory_space=pltpu.SMEM)
NT = (((1,), (1,)), ((), ()))
TN = (((0,), (0,)), ((), ()))


def place():
    ctx = lax.axis_index("ctx")
    return ctx // NJ, lax.rem(ctx, NJ), lax.axis_index("head")


def head_peer(i, j, h, d):
    return {"ctx": i * NJ + j, "head": lax.rem(h + d, HEADS)}


def x_peer(i, j, h, d):
    return {"ctx": lax.rem(i + d, NX) * NJ + j, "head": h}


def greet(peers):
    barrier = pltpu.get_barrier_semaphore()
    for peer in peers:
        pl.semaphore_signal(barrier, inc=1, device_id=peer, device_id_type=MESH)
    pl.semaphore_wait(barrier, len(peers))


def remote(src, dst, send, recv, peer):
    return pltpu.make_async_remote_copy(
        src_ref=src, dst_ref=dst, send_sem=send, recv_sem=recv, device_id=peer, device_id_type=MESH
    )


def cols(index, width):
    return pl.ds(pl.multiple_of(index * width, width), width)


def z_peer(i, j, h):
    return {"ctx": i * NJ + lax.rem(j + NY, NJ), "head": h}


def y_peer(i, j, h, d):
    return {"ctx": i * NJ + (j // NY) * NY + lax.rem(lax.rem(j, NY) + d + NY, NY), "head": h}


def ring_block(j, zc, d):
    other = lax.rem(j // NY + zc, 2)
    return other * NY + lax.rem(lax.rem(j, NY) + d + 2 * NY, NY)


def all_peers(i, j, h):
    return (
        [head_peer(i, j, h, d) for d in range(1, HEADS)]
        + [x_peer(i, j, h, d) for d in range(1, NX)]
        + [z_peer(i, j, h), y_peer(i, j, h, 1), y_peer(i, j, h, -1)]
    )


def query_positions(spans):
    i, j, h = place()
    lane = lax.broadcasted_iota(jnp.int32, (1, BLOCK), 1)
    rows = []
    for x in range(NX):
        at = 2 * (x * NJ + j)
        start = jnp.where(lane < CH, spans[at] * CH, spans[at + 1] * CH - CH)
        rows.append(start + lane)
    return jnp.concatenate(rows, axis=1)


def extra_row(extra_ref, n):
    return jnp.concatenate([extra_ref[8 * x + n : 8 * x + n + 1, :] for x in range(NX)], axis=1)


def masked_scores(spans, starts, qpos, key_block, query_head):
    scores = lax.dot_general(key_block, query_head, NT, preferred_element_type=jnp.float32)
    row = lax.broadcasted_iota(jnp.int32, (CH, QT), 0) - qpos
    parts = [
        jnp.where(row <= -CH * spans[at], scores[n * CH : (n + 1) * CH], LOW)
        for n, at in enumerate(starts)
    ]
    return jnp.concatenate(parts, axis=0)


def attention_kernel(
    spans, q_ref, g_ref, k_ref, v_ref, e_ref, oq, ok, ov,
    qa, ga, ka, va, ea, ep, st, sa, acc, dq, dk, dv, rq, rr, run, zs, zr, sq, sk, sv,
    local_sem, send1, recv1, send2, recv2, send3, recv3, send4, recv4, send5, recv5,
    send6, recv6, send7, recv7, send8, recv8, send9, recv9, out_sem, send10, recv10,
):
    i, j, h = place()
    zh, core = h // 2, lax.rem(h, 2)
    greet(all_peers(i, j, h))
    sent = []

    def push(src, dst, send, recv, peer):
        copy = remote(src, dst, send, recv, peer)
        copy.start()
        sent.append(copy)
        return copy

    ways = (1, -1)
    x_ways = (1, NX - 1)

    near_first = (1, 2, 3, 6, 7, 4, 5)

    def rank(at):
        return lax.rem(zh + at // 2, 4) * 2 + lax.rem(core + at % 2, 2)

    def pieces(c):
        mine_q = cols(i * HEADS + h, OWN)
        mine_k = cols(j * HEADS + h, OWN)
        return [
            (k_ref.at[:, cols(c, WIDTH)], ka.at[mine_k, :]),
            (v_ref.at[:, cols(c, WIDTH)], va.at[mine_k, :]),
            (e_ref.at[cols(c, 8), :], ep.at[cols(h, 8), :]),
            (q_ref.at[:, cols(c, GROUP * WIDTH)], qa.at[mine_q, :]),
            (g_ref.at[:, cols(c, GROUP * WIDTH)], ga.at[mine_q, :]),
        ]

    first = {}
    for kinds in ((0, 1), (2, 3, 4)):
        for at in near_first:
            c = rank(at)
            for n in kinds:
                src, dst = pieces(c)[n]
                peer = {"ctx": i * NJ + j, "head": c}
                first[at, n] = push(src, dst, send1.at[at, n], recv1.at[at, n], peer)
    own = []
    for n, (src, dst) in enumerate(pieces(h)):
        copy = pltpu.make_async_copy(src, dst, local_sem.at[n])
        copy.start()
        own.append(copy)
    for copy in own:
        copy.wait()

    pair = (ka, va)
    ring = {}

    def spread(ref, rows, send, recv, peer):
        return push(ref.at[rows, :], ref.at[rows, :], send, recv, peer)

    def ring_push(step, zc, way, kinds):
        rows = cols(ring_block(j, zc, -ways[way] * (step - 1)), BLOCK)
        for n in kinds:
            at = (way, step - 1, zc, n)
            ring[way, step, zc, n] = spread(
                pair[n], rows, send3.at[at], recv3.at[at], y_peer(i, j, h, ways[way])
            )

    def ring_step(step):
        for zc in range(2):
            for way in range(2):
                for n in range(2):
                    ring[way, step - 1, zc, n].wait_recv()
                ring_push(step, zc, way, (0, 1) if step < 4 else (way,))

    x_first, x_last = {}, {}

    def x_start(dz):
        for dc in range(2):
            if dz or dc:
                for n in (3, 4):
                    first[2 * dz + dc, n].wait_recv()
        rows = cols(i * 4 + lax.rem(zh - dz + 4, 4), 2 * OWN)
        for way in range(2):
            for n, ref in enumerate((qa, ga)):
                at = (way, 0, n, dz)
                x_first[way, n, dz] = spread(
                    ref, rows, send2.at[at], recv2.at[at], x_peer(i, j, h, x_ways[way])
                )

    def x_relay(dz):
        for way, ref in enumerate((qa, ga)):
            x_first[way, way, dz].wait_recv()
            x = lax.rem(i - ways[way] + NX, NX)
            rows = cols(x * 4 + lax.rem(zh - dz + 4, 4), 2 * OWN)
            at = (way, 1, way, dz)
            x_last[way, dz] = spread(
                ref, rows, send2.at[at], recv2.at[at], x_peer(i, j, h, x_ways[way])
            )

    for n in range(2):
        for at in near_first:
            first[at, n].wait_recv()
    across = [
        spread(pair[n], cols(j, BLOCK), send4.at[n], recv4.at[n], z_peer(i, j, h))
        for n in range(2)
    ]
    for way in range(2):
        ring_push(1, 0, way, (0, 1))
    x_start(0)
    for copy in across:
        copy.wait_recv()
    for way in range(2):
        ring_push(1, 1, way, (0, 1))
    x_start(1)
    x_start(3)
    ring_step(2)
    x_relay(0)
    x_start(2)
    for at in near_first:
        first[at, 2].wait_recv()
    ea[cols(i, 8), :] = jnp.concatenate(
        [ep[8 * n : 8 * n + 8, :OWN] for n in range(HEADS)], axis=1
    )
    extras = [
        spread(ea, cols(i, 8), send5.at[d], recv5.at[d], x_peer(i, j, h, d)) for d in range(1, NX)
    ]
    ring_step(3)
    x_relay(1)
    x_relay(3)
    ring_step(4)
    x_relay(2)
    for zc in range(2):
        for way in range(2):
            ring[way, 4, zc, way].wait_recv()
    for dz in range(4):
        for way in range(2):
            x_first[way, 1 - way, dz].wait_recv()
            x_last[way, dz].wait_recv()
    for copy in extras:
        copy.wait_recv()

    qpos = query_positions(spans)
    first_span = i * (KT // CH)

    def stats_step(b, carry):
        key_block = ka[pl.ds(pl.multiple_of(b * KB, KB), KB), :]
        starts = [first_span + b * (KB // CH) + n for n in range(KB // CH)]
        following = []
        for g in range(GROUP):
            top, total = carry[g]
            scores = masked_scores(
                spans, starts, qpos, key_block, qa[:, g * WIDTH : (g + 1) * WIDTH]
            )
            new_top = jnp.maximum(top, jnp.max(scores, axis=0, keepdims=True))
            total = total * jnp.exp2((top - new_top) * SCALE2) + jnp.sum(
                jnp.exp2((scores - new_top) * SCALE2), axis=0, keepdims=True
            )
            following.append((new_top, total))
        return tuple(following)

    start = tuple(
        (jnp.full((1, QT), FLOOR, jnp.float32), jnp.zeros((1, QT), jnp.float32))
        for g in range(GROUP)
    )
    result = lax.fori_loop(0, KT // KB, stats_step, start)
    st[...] = jnp.concatenate([r[0] for r in result] + [r[1] for r in result], axis=0)
    shared = [
        push(st, sa.at[d - 1], send6.at[d], recv6.at[d], x_peer(i, j, h, d)) for d in range(1, NX)
    ]
    gain = extra_row(ea, GROUP)
    gain_scale = gain * SCALE
    out_dots = [extra_row(ea, g) for g in range(GROUP)]
    acc[...] = jnp.zeros_like(acc)
    for copy in shared:
        copy.wait_recv()
    blocks = [st[...]] + [sa[d] for d in range(NX - 1)]
    top = functools.reduce(jnp.maximum, [b[:GROUP] for b in blocks])
    total = sum(b[GROUP:] * jnp.exp2((b[:GROUP] - top) * SCALE2) for b in blocks)
    norm_rows = top * SCALE2 + jnp.log2(total)
    norms = [norm_rows[g : g + 1] for g in range(GROUP)]

    def grads_of(d):
        owners = [ring_block(j, zc, d) for zc in range(2)]
        rows = [cols(owner, BLOCK) for owner in owners]
        key_block = jnp.concatenate([ka[r, :] for r in rows], axis=0)
        value_block = jnp.concatenate([va[r, :] for r in rows], axis=0)
        starts = [first_span + owner * 2 + n for owner in owners for n in range(2)]
        key_grad = jnp.zeros((2 * BLOCK, WIDTH), jnp.float32)
        value_grad = jnp.zeros((2 * BLOCK, WIDTH), jnp.float32)
        for g in range(GROUP):
            part = slice(g * WIDTH, (g + 1) * WIDTH)
            query_head = qa[:, part]
            grad_head = ga[:, part]
            scores = masked_scores(spans, starts, qpos, key_block, query_head)
            probs = jnp.exp2(scores * SCALE2 - norms[g])
            prob_grads = lax.dot_general(
                value_block, grad_head, NT, preferred_element_type=jnp.float32
            )
            weighted = (probs * gain).astype(jnp.bfloat16)
            score_grads = (probs * ((prob_grads - out_dots[g]) * gain_scale)).astype(jnp.bfloat16)
            key_grad += jnp.dot(score_grads, query_head, preferred_element_type=jnp.float32)
            value_grad += jnp.dot(weighted, grad_head, preferred_element_type=jnp.float32)
            acc[:, part] += lax.dot_general(
                score_grads, key_block, TN, preferred_element_type=jnp.float32
            )
        for zc in range(2):
            dk[rows[zc], :] = key_grad[zc * BLOCK : (zc + 1) * BLOCK].astype(jnp.bfloat16)
            dv[rows[zc], :] = value_grad[zc * BLOCK : (zc + 1) * BLOCK].astype(jnp.bfloat16)

    partial = (dk, dv)
    back = {}

    def back_push(src, way, step, zc, n):
        at = (way, step - 1, zc, n)
        back[way, step, zc, n] = push(
            src, rr.at[at], send7.at[at], recv7.at[at], y_peer(i, j, h, ways[way])
        )

    def target(way, step, zc):
        return cols(ring_block(j, zc, ways[way] * (5 - step)), BLOCK)

    def back_step(way, step):
        for zc in (1, 0):
            if step == 2:
                src = partial[1 - way].at[target(way, 2, zc), :]
                back_push(src, way, 2, zc, 1 - way)
            for n in range(2) if step > 2 else (way,):
                back[way, step - 1, zc, n].wait_recv()
                total = rr[way, step - 2, zc, n].astype(jnp.float32) + partial[n][
                    target(way, step, zc), :
                ].astype(jnp.float32)
                run[way, step - 2, zc, n] = total.astype(jnp.bfloat16)
                back_push(run.at[way, step - 2, zc, n], way, step, zc, n)

    grads_of(4)
    for zc in (1, 0):
        for way in range(2):
            back_push(partial[way].at[target(way, 1, zc), :], way, 1, zc, way)
    for step in range(2, 5):
        for way in range(2):
            grads_of(ways[way] * (5 - step))
            back_step(way, step)
    grads_of(0)
    dq[...] = acc[...].astype(jnp.bfloat16)
    query_parts = []
    for d in range(1, NX):
        rows = cols(lax.rem(i + d, NX), BLOCK)
        query_parts.append(
            push(dq.at[rows, :], rq.at[d - 1], send8.at[d], recv8.at[d], x_peer(i, j, h, d))
        )

    def ring_total(zc, n):
        for way in range(2):
            back[way, 4, zc, n].wait_recv()
        rows = cols(ring_block(j, zc, 0), BLOCK)
        return (
            partial[n][rows, :].astype(jnp.float32)
            + rr[0, 3, zc, n].astype(jnp.float32)
            + rr[1, 3, zc, n].astype(jnp.float32)
        )

    over = []
    for n in range(2):
        zs[n] = ring_total(1, n).astype(jnp.bfloat16)
        over.append(push(zs.at[n], zr.at[n], send9.at[n], recv9.at[n], z_peer(i, j, h)))
    for n, out in enumerate((sk, sv)):
        total = ring_total(0, n)
        over[n].wait_recv()
        out[...] = (total + zr[n].astype(jnp.float32)).astype(jnp.bfloat16)

    def finished(c):
        rows = cols(c, OWN)
        return [
            (sk.at[rows, :], ok.at[:, cols(h, WIDTH)]),
            (sv.at[rows, :], ov.at[:, cols(h, WIDTH)]),
            (sq.at[rows, :], oq.at[:, cols(h, GROUP * WIDTH)]),
        ]

    last = []

    def give(kinds):
        for at in (4, 5, 2, 3, 6, 7, 1):
            c = rank(at)
            for n in kinds:
                src, dst = finished(c)[n]
                peer = {"ctx": i * NJ + j, "head": c}
                last.append(push(src, dst, send10.at[at, n], recv10.at[at, n], peer))
        for n in kinds:
            src, dst = finished(h)[n]
            copy = pltpu.make_async_copy(src, dst, out_sem.at[n])
            copy.start()
            kept.append(copy)

    kept = []
    give((0, 1))
    for copy in query_parts:
        copy.wait_recv()
    total = dq[cols(i, BLOCK), :].astype(jnp.float32)
    for d in range(1, NX):
        total += rq[d - 1].astype(jnp.float32)
    sq[...] = total.astype(jnp.bfloat16)
    give((2,))
    for copy in kept:
        copy.wait()
    for copy in last:
        copy.wait_recv()
    for copy in sent:
        copy.wait_send()


def attention(spans, queries, grads, keys, values, extra):
    dma = pltpu.SemaphoreType.DMA
    bf16, f32 = jnp.bfloat16, jnp.float32
    vmem = pltpu.VMEM

    def both(*shape):
        return [dma(shape), dma(shape)]

    return pl.pallas_call(
        attention_kernel,
        out_shape=(
            jax.ShapeDtypeStruct((OWN, QUERY_HEADS * WIDTH), bf16),
            jax.ShapeDtypeStruct((OWN, KEY_VALUE_HEADS * WIDTH), bf16),
            jax.ShapeDtypeStruct((OWN, KEY_VALUE_HEADS * WIDTH), bf16),
        ),
        in_specs=[SMEM] + [VMEM] * 5,
        out_specs=[VMEM] * 3,
        scratch_shapes=[
            vmem((QT, GROUP * WIDTH), bf16),
            vmem((QT, GROUP * WIDTH), bf16),
            vmem((KT, WIDTH), bf16),
            vmem((KT, WIDTH), bf16),
            vmem((NX * 8, 128), f32),
            vmem((HEADS * 8, 128), f32),
            vmem((2 * GROUP, QT), f32),
            vmem((NX - 1, 2 * GROUP, QT), f32),
            vmem((QT, GROUP * WIDTH), f32),
            vmem((QT, GROUP * WIDTH), bf16),
            vmem((KT, WIDTH), bf16),
            vmem((KT, WIDTH), bf16),
            vmem((NX - 1, BLOCK, GROUP * WIDTH), bf16),
            vmem((2, 4, 2, 2, BLOCK, WIDTH), bf16),
            vmem((2, 3, 2, 2, BLOCK, WIDTH), bf16),
            vmem((2, BLOCK, WIDTH), bf16),
            vmem((2, BLOCK, WIDTH), bf16),
            vmem((BLOCK, GROUP * WIDTH), bf16),
            vmem((BLOCK, WIDTH), bf16),
            vmem((BLOCK, WIDTH), bf16),
            dma((5,)),
        ]
        + both(HEADS, 5)
        + both(2, 2, 2, 4)
        + both(2, 4, 2, 2)
        + both(2)
        + both(NX)
        + both(NX)
        + both(2, 4, 2, 2)
        + both(NX)
        + both(2)
        + [dma((3,))]
        + both(HEADS, 3),
        compiler_params=pltpu.CompilerParams(collective_id=0, has_side_effects=True),
        name="attention",
    )(spans, queries, grads, keys, values, extra)


def on_device(queries, keys, values, outputs, output_gradient, importance, span_order):
    i, j, h = place()
    out_dot = jnp.sum(
        (output_gradient.astype(jnp.float32) * outputs.astype(jnp.float32)).reshape(
            OWN, KEY_VALUE_HEADS, GROUP, WIDTH
        ),
        axis=-1,
    ).transpose(1, 2, 0)
    own_gain = lax.dynamic_slice_in_dim(importance.astype(jnp.float32) * 0.25, h * OWN, OWN)
    extra = jnp.concatenate(
        [out_dot, jnp.broadcast_to(own_gain, (KEY_VALUE_HEADS, 1, OWN))], axis=1
    )
    extra = jnp.pad(extra, ((0, 0), (0, 8 - GROUP - 1), (0, 128 - OWN)))
    return attention(
        span_order, queries, output_gradient, keys, values, extra.reshape(KEY_VALUE_HEADS * 8, 128)
    )


def solution(mesh):
    tokens = P(("ctx", "head"), None)
    return jax.shard_map(
        on_device,
        mesh=mesh,
        in_specs=(tokens, tokens, tokens, tokens, tokens, P("ctx"), P()),
        out_specs=(tokens, tokens, tokens),
        check_vma=False,
    )
```

```python
import functools
import math

import jax
import jax.numpy as jnp
from jax import lax
from jax.experimental import pallas as pl
from jax.experimental.pallas import tpu as pltpu
from jax.sharding import PartitionSpec as P

QUERY_HEADS = 32
KEY_VALUE_HEADS = 8
GROUP = 4
WIDTH = 128
CH = 64
HEADS = 8
NX = 4
NJ = 16
NY = 8
OWN = 16
BLOCK = 128
QT = NX * BLOCK
KT = NJ * BLOCK
KB = 512
SCALE = 1.0 / math.sqrt(WIDTH)
SCALE2 = SCALE * math.log2(math.e)
LOW = -1e30
FLOOR = -1e20

MESH = pl.DeviceIdType.MESH
VMEM = pl.BlockSpec(memory_space=pltpu.VMEM)
SMEM = pl.BlockSpec(memory_space=pltpu.SMEM)
NT = (((1,), (1,)), ((), ()))
TN = (((0,), (0,)), ((), ()))


def place():
    ctx = lax.axis_index("ctx")
    return ctx // NJ, lax.rem(ctx, NJ), lax.axis_index("head")


def head_peer(i, j, h, d):
    return {"ctx": i * NJ + j, "head": lax.rem(h + d, HEADS)}


def x_peer(i, j, h, d):
    return {"ctx": lax.rem(i + d, NX) * NJ + j, "head": h}


def announce(peers):
    for peer in peers:
        pl.semaphore_signal(
            pltpu.get_barrier_semaphore(), inc=1, device_id=peer, device_id_type=MESH
        )


def remote(src, dst, send, recv, peer):
    return pltpu.make_async_remote_copy(
        src_ref=src, dst_ref=dst, send_sem=send, recv_sem=recv, device_id=peer, device_id_type=MESH
    )


def cols(index, width):
    return pl.ds(pl.multiple_of(index * width, width), width)


def z_peer(i, j, h):
    return {"ctx": i * NJ + lax.rem(j + NY, NJ), "head": h}


def y_peer(i, j, h, d):
    return {"ctx": i * NJ + (j // NY) * NY + lax.rem(lax.rem(j, NY) + d + NY, NY), "head": h}


def ring_block(j, zc, d):
    other = lax.rem(j // NY + zc, 2)
    return other * NY + lax.rem(lax.rem(j, NY) + d + 2 * NY, NY)


def all_peers(i, j, h):
    return (
        [head_peer(i, j, h, d) for d in range(1, HEADS)]
        + [x_peer(i, j, h, d) for d in range(1, NX)]
        + [z_peer(i, j, h), y_peer(i, j, h, 1), y_peer(i, j, h, -1)]
    )


def block_positions(spans, x, j):
    lane = lax.broadcasted_iota(jnp.int32, (1, BLOCK), 1)
    at = 2 * (x * NJ + j)
    return jnp.where(lane < CH, spans[at] * CH, spans[at + 1] * CH - CH) + lane


def extra_row(extra_ref, n):
    return jnp.concatenate([extra_ref[8 * x + n : 8 * x + n + 1, :] for x in range(NX)], axis=1)


def masked_scores(spans, starts, qpos, key_block, query_head):
    scores = lax.dot_general(key_block, query_head, NT, preferred_element_type=jnp.float32)
    row = lax.broadcasted_iota(jnp.int32, (CH, QT), 0) - qpos
    parts = [
        jnp.where(row <= -CH * spans[at], scores[n * CH : (n + 1) * CH], LOW)
        for n, at in enumerate(starts)
    ]
    return jnp.concatenate(parts, axis=0)


def attention_kernel(
    spans, q_ref, g_ref, k_ref, v_ref, o_ref, w_ref, oq, ok, ov,
    e_ref, qa, ga, ka, va, ea, ep, st, sa, acc, dq, dk, dv, rq, rr, run, zs, zr, sq, sk, sv,
    local_sem, send1, recv1, send2, recv2, send3, recv3, send4, recv4, send5, recv5,
    send6, recv6, send7, recv7, send8, recv8, send9, recv9, out_sem, send10, recv10,
):
    i, j, h = place()
    zh, core = h // 2, lax.rem(h, 2)
    peers = all_peers(i, j, h)
    announce(peers)

    lane_head = lax.broadcasted_iota(jnp.int32, (8, GROUP * WIDTH), 1) // WIDTH
    pick = (lane_head == lax.broadcasted_iota(jnp.int32, (8, GROUP * WIDTH), 0)).astype(jnp.float32)
    for c in range(KEY_VALUE_HEADS):
        part = slice(c * GROUP * WIDTH, (c + 1) * GROUP * WIDTH)
        product = g_ref[:, part].astype(jnp.float32) * o_ref[:, part].astype(jnp.float32)
        sums = lax.dot_general(
            pick, product, NT, precision=lax.Precision.HIGHEST, preferred_element_type=jnp.float32
        )
        e_ref[8 * c : 8 * c + 8, :] = jnp.concatenate(
            [sums, jnp.zeros((8, 128 - OWN), jnp.float32)], axis=1
        )
    pl.semaphore_wait(pltpu.get_barrier_semaphore(), len(peers))
    sent = []

    def push(src, dst, send, recv, peer):
        copy = remote(src, dst, send, recv, peer)
        copy.start()
        sent.append(copy)
        return copy

    ways = (1, -1)
    x_ways = (1, NX - 1)

    near_first = (1, 2, 3, 6, 7, 4, 5)

    def rank(at):
        return lax.rem(zh + at // 2, 4) * 2 + lax.rem(core + at % 2, 2)

    def pieces(c):
        mine_q = cols(i * HEADS + h, OWN)
        mine_k = cols(j * HEADS + h, OWN)
        return [
            (k_ref.at[:, cols(c, WIDTH)], ka.at[mine_k, :]),
            (v_ref.at[:, cols(c, WIDTH)], va.at[mine_k, :]),
            (e_ref.at[cols(c, 8), :], ep.at[cols(h, 8), :]),
            (q_ref.at[:, cols(c, GROUP * WIDTH)], qa.at[mine_q, :]),
            (g_ref.at[:, cols(c, GROUP * WIDTH)], ga.at[mine_q, :]),
        ]

    first = {}
    for kinds in ((0, 1), (2, 3, 4)):
        for at in near_first:
            c = rank(at)
            for n in kinds:
                src, dst = pieces(c)[n]
                peer = {"ctx": i * NJ + j, "head": c}
                first[at, n] = push(src, dst, send1.at[at, n], recv1.at[at, n], peer)
    own = []
    for n, (src, dst) in enumerate(pieces(h)):
        copy = pltpu.make_async_copy(src, dst, local_sem.at[n])
        copy.start()
        own.append(copy)
    for copy in own:
        copy.wait()

    pair = (ka, va)
    ring = {}

    def spread(ref, rows, send, recv, peer):
        return push(ref.at[rows, :], ref.at[rows, :], send, recv, peer)

    def ring_push(step, zc, way, kinds):
        rows = cols(ring_block(j, zc, -ways[way] * (step - 1)), BLOCK)
        for n in kinds:
            at = (way, step - 1, zc, n)
            ring[way, step, zc, n] = spread(
                pair[n], rows, send3.at[at], recv3.at[at], y_peer(i, j, h, ways[way])
            )

    def ring_step(step):
        for zc in range(2):
            for way in range(2):
                for n in range(2):
                    ring[way, step - 1, zc, n].wait_recv()
                ring_push(step, zc, way, (0, 1) if step < 4 else (way,))

    x_first, x_last = {}, {}

    def x_start(dz):
        for dc in range(2):
            if dz or dc:
                for n in (3, 4):
                    first[2 * dz + dc, n].wait_recv()
        rows = cols(i * 4 + lax.rem(zh - dz + 4, 4), 2 * OWN)
        for way in range(2):
            for n, ref in enumerate((qa, ga)):
                at = (way, 0, n, dz)
                x_first[way, n, dz] = spread(
                    ref, rows, send2.at[at], recv2.at[at], x_peer(i, j, h, x_ways[way])
                )

    def x_relay(dz):
        for way, ref in enumerate((qa, ga)):
            x_first[way, way, dz].wait_recv()
            x = lax.rem(i - ways[way] + NX, NX)
            rows = cols(x * 4 + lax.rem(zh - dz + 4, 4), 2 * OWN)
            at = (way, 1, way, dz)
            x_last[way, dz] = spread(
                ref, rows, send2.at[at], recv2.at[at], x_peer(i, j, h, x_ways[way])
            )

    for n in range(2):
        for at in near_first:
            first[at, n].wait_recv()
    across = [
        spread(pair[n], cols(j, BLOCK), send4.at[n], recv4.at[n], z_peer(i, j, h))
        for n in range(2)
    ]
    for way in range(2):
        ring_push(1, 0, way, (0, 1))
    x_start(0)
    for copy in across:
        copy.wait_recv()
    for way in range(2):
        ring_push(1, 1, way, (0, 1))
    x_start(1)
    x_start(3)
    ring_step(2)
    x_relay(0)
    x_start(2)
    for at in near_first:
        first[at, 2].wait_recv()
    own_extra = jnp.concatenate([ep[8 * n : 8 * n + 8, :OWN] for n in range(HEADS)], axis=1)
    own_gain = w_ref[...].astype(jnp.float32) * 0.25
    extra_at = lax.broadcasted_iota(jnp.int32, (8, BLOCK), 0)
    ea[cols(i, 8), :] = jnp.where(extra_at == GROUP, own_gain, own_extra)
    extras = [
        spread(ea, cols(i, 8), send5.at[d], recv5.at[d], x_peer(i, j, h, d)) for d in range(1, NX)
    ]
    ring_step(3)
    x_relay(1)
    x_relay(3)
    ring_step(4)
    x_relay(2)
    for zc in range(2):
        for way in range(2):
            ring[way, 4, zc, way].wait_recv()
    first_span = i * (KT // CH)

    def stats_of(x):
        rows = cols(x, BLOCK)
        block = jnp.concatenate(
            [qa[rows, g * WIDTH : (g + 1) * WIDTH] for g in range(GROUP)], axis=0
        )
        positions = jnp.concatenate([block_positions(spans, x, j)] * GROUP, axis=1)

        def merge(one, two):
            top = jnp.maximum(one[0], two[0])
            return top, one[1] * jnp.exp2((one[0] - top) * SCALE2) + two[1] * jnp.exp2(
                (two[0] - top) * SCALE2
            )

        def stats_step(b, carry):
            following = []
            for half in range(2):
                at = 2 * b + half
                key_block = ka[pl.ds(pl.multiple_of(at * KB, KB), KB), :]
                starts = [first_span + at * (KB // CH) + n for n in range(KB // CH)]
                scores = masked_scores(spans, starts, positions, key_block, block)
                top = jnp.maximum(FLOOR, jnp.max(scores, axis=0, keepdims=True))
                total = jnp.sum(jnp.exp2((scores - top) * SCALE2), axis=0, keepdims=True)
                following.append(merge(carry[half], (top, total)))
            return tuple(following)

        nothing = (
            jnp.full((1, GROUP * BLOCK), FLOOR, jnp.float32),
            jnp.zeros((1, GROUP * BLOCK), jnp.float32),
        )
        halves = lax.fori_loop(0, KT // KB // 2, stats_step, (nothing, nothing))
        found = merge(*halves)
        st[:, rows] = jnp.concatenate(
            [r[:, g * BLOCK : (g + 1) * BLOCK] for r in found for g in range(GROUP)], axis=0
        )

    for dz in range(4):
        x_first[1, 0, dz].wait_recv()

    def early(t, carry):
        stats_of(lax.rem(i + 3 + t, NX))
        return carry

    lax.fori_loop(0, 3, early, 0)
    for dz in range(4):
        x_last[0, dz].wait_recv()
    stats_of(lax.rem(i + 2, NX))
    shared = [
        push(st, sa.at[d - 1], send6.at[d], recv6.at[d], x_peer(i, j, h, d)) for d in range(1, NX)
    ]
    for dz in range(4):
        x_first[0, 1, dz].wait_recv()
        x_last[1, dz].wait_recv()
    for copy in extras:
        copy.wait_recv()
    qpos = jnp.concatenate([block_positions(spans, x, j) for x in range(NX)], axis=1)
    gain = extra_row(ea, GROUP)
    gain_scale = gain * SCALE
    out_dots = [extra_row(ea, g) for g in range(GROUP)]
    acc[...] = jnp.zeros_like(acc)
    for copy in shared:
        copy.wait_recv()
    blocks = [st[...]] + [sa[d] for d in range(NX - 1)]
    top = functools.reduce(jnp.maximum, [b[:GROUP] for b in blocks])
    total = sum(b[GROUP:] * jnp.exp2((b[:GROUP] - top) * SCALE2) for b in blocks)
    norm_rows = top * SCALE2 + jnp.log2(total)
    norms = [norm_rows[g : g + 1] for g in range(GROUP)]

    query_parts = {}

    def grads_of(distances, closing=False):
        owners = [ring_block(j, zc, d) for d in distances for zc in range(2)]
        rows = [cols(owner, BLOCK) for owner in owners]
        key_block = jnp.concatenate([ka[r, :] for r in rows], axis=0)
        value_block = jnp.concatenate([va[r, :] for r in rows], axis=0)
        starts = [first_span + owner * 2 + n for owner in owners for n in range(2)]
        key_grad = jnp.zeros((len(owners) * BLOCK, WIDTH), jnp.float32)
        value_grad = jnp.zeros((len(owners) * BLOCK, WIDTH), jnp.float32)
        for g in range(GROUP):
            part = slice(g * WIDTH, (g + 1) * WIDTH)
            query_head = qa[:, part]
            grad_head = ga[:, part]
            scores = masked_scores(spans, starts, qpos, key_block, query_head)
            probs = jnp.exp2(scores * SCALE2 - norms[g])
            prob_grads = lax.dot_general(
                value_block, grad_head, NT, preferred_element_type=jnp.float32
            )
            weighted = (probs * gain).astype(jnp.bfloat16)
            score_grads = (probs * ((prob_grads - out_dots[g]) * gain_scale)).astype(jnp.bfloat16)
            query_term = lax.dot_general(
                score_grads, key_block, TN, preferred_element_type=jnp.float32
            )
            if closing:
                dq[g] = (acc[:, part] + query_term).astype(jnp.bfloat16)
                for d in range(1, NX):
                    query_parts[d, g] = push(
                        dq.at[g, cols(lax.rem(i + d, NX), BLOCK), :],
                        rq.at[d - 1, g],
                        send8.at[d, g],
                        recv8.at[d, g],
                        x_peer(i, j, h, d),
                    )
            else:
                acc[:, part] += query_term
            key_grad += jnp.dot(score_grads, query_head, preferred_element_type=jnp.float32)
            value_grad += jnp.dot(weighted, grad_head, preferred_element_type=jnp.float32)
        for n, r in enumerate(rows):
            dk[r, :] = key_grad[n * BLOCK : (n + 1) * BLOCK].astype(jnp.bfloat16)
            dv[r, :] = value_grad[n * BLOCK : (n + 1) * BLOCK].astype(jnp.bfloat16)

    partial = (dk, dv)
    back = {}

    def back_push(src, way, step, zc, n):
        at = (way, step - 1, zc, n)
        back[way, step, zc, n] = push(
            src, rr.at[at], send7.at[at], recv7.at[at], y_peer(i, j, h, ways[way])
        )

    def target(way, step, zc):
        return cols(ring_block(j, zc, ways[way] * (5 - step)), BLOCK)

    def back_step(way, step):
        for zc in (1, 0):
            if step == 2:
                src = partial[1 - way].at[target(way, 2, zc), :]
                back_push(src, way, 2, zc, 1 - way)
            for n in range(2) if step > 2 else (way,):
                back[way, step - 1, zc, n].wait_recv()
                total = rr[way, step - 2, zc, n].astype(jnp.float32) + partial[n][
                    target(way, step, zc), :
                ].astype(jnp.float32)
                run[way, step - 2, zc, n] = total.astype(jnp.bfloat16)
                back_push(run.at[way, step - 2, zc, n], way, step, zc, n)

    grads_of((4,))
    for zc in (1, 0):
        for way in range(2):
            back_push(partial[way].at[target(way, 1, zc), :], way, 1, zc, way)
    for step in (2, 3):
        for way in range(2):
            grads_of((ways[way] * (5 - step),))
            back_step(way, step)
    grads_of((1,))
    back_step(0, 4)
    grads_of((-1, 0), closing=True)
    back_step(1, 4)

    def ring_total(zc, n):
        for way in range(2):
            back[way, 4, zc, n].wait_recv()
        rows = cols(ring_block(j, zc, 0), BLOCK)
        return (
            partial[n][rows, :].astype(jnp.float32)
            + rr[0, 3, zc, n].astype(jnp.float32)
            + rr[1, 3, zc, n].astype(jnp.float32)
        )

    last, kept = [], []

    def give(n, source, out):
        for at in (4, 5, 2, 3, 6, 7, 1):
            c = rank(at)
            peer = {"ctx": i * NJ + j, "head": c}
            src = source.at[cols(c, OWN), :]
            last.append(push(src, out, send10.at[at, n], recv10.at[at, n], peer))
        copy = pltpu.make_async_copy(source.at[cols(h, OWN), :], out, out_sem.at[n])
        copy.start()
        kept.append(copy)

    def give_queries(g):
        total = dq[g, cols(i, BLOCK), :].astype(jnp.float32)
        for d in range(1, NX):
            query_parts[d, g].wait_recv()
            total += rq[d - 1, g].astype(jnp.float32)
        sq[g] = total.astype(jnp.bfloat16)
        give(g, sq.at[g], oq.at[:, cols(h * GROUP + g, WIDTH)])

    give_queries(0)
    over = []
    for n in range(2):
        zs[n] = ring_total(1, n).astype(jnp.bfloat16)
        over.append(push(zs.at[n], zr.at[n], send9.at[n], recv9.at[n], z_peer(i, j, h)))
    give_queries(1)
    give_queries(2)
    for n, (held, out) in enumerate(((sk, ok), (sv, ov))):
        total = ring_total(0, n)
        over[n].wait_recv()
        held[...] = (total + zr[n].astype(jnp.float32)).astype(jnp.bfloat16)
        give(GROUP + n, held, out.at[:, cols(h, WIDTH)])
    give_queries(3)
    for copy in kept:
        copy.wait()
    for copy in last:
        copy.wait_recv()
    for copy in sent:
        copy.wait_send()


def attention(spans, queries, grads, keys, values, outputs, importance):
    dma = pltpu.SemaphoreType.DMA
    bf16, f32 = jnp.bfloat16, jnp.float32
    vmem = pltpu.VMEM

    def both(*shape):
        return [dma(shape), dma(shape)]

    return pl.pallas_call(
        attention_kernel,
        out_shape=(
            jax.ShapeDtypeStruct((OWN, QUERY_HEADS * WIDTH), bf16),
            jax.ShapeDtypeStruct((OWN, KEY_VALUE_HEADS * WIDTH), bf16),
            jax.ShapeDtypeStruct((OWN, KEY_VALUE_HEADS * WIDTH), bf16),
        ),
        in_specs=[SMEM] + [VMEM] * 6,
        out_specs=[VMEM] * 3,
        scratch_shapes=[
            vmem((KEY_VALUE_HEADS * 8, 128), f32),
            vmem((QT, GROUP * WIDTH), bf16),
            vmem((QT, GROUP * WIDTH), bf16),
            vmem((KT, WIDTH), bf16),
            vmem((KT, WIDTH), bf16),
            vmem((NX * 8, 128), f32),
            vmem((HEADS * 8, 128), f32),
            vmem((2 * GROUP, QT), f32),
            vmem((NX - 1, 2 * GROUP, QT), f32),
            vmem((QT, GROUP * WIDTH), f32),
            vmem((GROUP, QT, WIDTH), bf16),
            vmem((KT, WIDTH), bf16),
            vmem((KT, WIDTH), bf16),
            vmem((NX - 1, GROUP, BLOCK, WIDTH), bf16),
            vmem((2, 4, 2, 2, BLOCK, WIDTH), bf16),
            vmem((2, 3, 2, 2, BLOCK, WIDTH), bf16),
            vmem((2, BLOCK, WIDTH), bf16),
            vmem((2, BLOCK, WIDTH), bf16),
            vmem((GROUP, BLOCK, WIDTH), bf16),
            vmem((BLOCK, WIDTH), bf16),
            vmem((BLOCK, WIDTH), bf16),
            dma((5,)),
        ]
        + both(HEADS, 5)
        + both(2, 2, 2, 4)
        + both(2, 4, 2, 2)
        + both(2)
        + both(NX)
        + both(NX)
        + both(2, 4, 2, 2)
        + both(NX, GROUP)
        + both(2)
        + [dma((GROUP + 2,))]
        + both(HEADS, GROUP + 2),
        compiler_params=pltpu.CompilerParams(collective_id=0, has_side_effects=True),
        name="attention",
    )(spans, queries, grads, keys, values, outputs, importance)


def on_device(queries, keys, values, outputs, output_gradient, importance, span_order):
    return attention(
        span_order, queries, output_gradient, keys, values, outputs, importance.reshape(1, BLOCK)
    )


def solution(mesh):
    tokens = P(("ctx", "head"), None)
    return jax.shard_map(
        on_device,
        mesh=mesh,
        in_specs=(tokens, tokens, tokens, tokens, tokens, P("ctx"), P()),
        out_specs=(tokens, tokens, tokens),
        check_vma=False,
    )
```

```python
import functools
import math

import jax
import jax.numpy as jnp
from jax import lax
from jax.experimental import pallas as pl
from jax.experimental.pallas import tpu as pltpu
from jax.sharding import PartitionSpec as P

QUERY_HEADS = 32
KEY_VALUE_HEADS = 8
GROUP = 4
WIDTH = 128
CH = 64
HEADS = 8
NX = 4
NJ = 16
NY = 8
OWN = 16
BLOCK = 128
QT = NX * BLOCK
KT = NJ * BLOCK
KB = 512
SCALE = 1.0 / math.sqrt(WIDTH)
SCALE2 = SCALE * math.log2(math.e)
LOW = -1e30
FLOOR = -1e20

MESH = pl.DeviceIdType.MESH
VMEM = pl.BlockSpec(memory_space=pltpu.VMEM)
SMEM = pl.BlockSpec(memory_space=pltpu.SMEM)
NT = (((1,), (1,)), ((), ()))
TN = (((0,), (0,)), ((), ()))


def place():
    ctx = lax.axis_index("ctx")
    return ctx // NJ, lax.rem(ctx, NJ), lax.axis_index("head")


def head_peer(i, j, h, d):
    return {"ctx": i * NJ + j, "head": lax.rem(h + d, HEADS)}


def x_peer(i, j, h, d):
    return {"ctx": lax.rem(i + d, NX) * NJ + j, "head": h}


def announce(peers):
    for peer in peers:
        pl.semaphore_signal(
            pltpu.get_barrier_semaphore(), inc=1, device_id=peer, device_id_type=MESH
        )


def remote(src, dst, send, recv, peer):
    return pltpu.make_async_remote_copy(
        src_ref=src, dst_ref=dst, send_sem=send, recv_sem=recv, device_id=peer, device_id_type=MESH
    )


def cols(index, width):
    return pl.ds(pl.multiple_of(index * width, width), width)


def z_peer(i, j, h):
    return {"ctx": i * NJ + lax.rem(j + NY, NJ), "head": h}


def y_peer(i, j, h, d):
    return {"ctx": i * NJ + (j // NY) * NY + lax.rem(lax.rem(j, NY) + d + NY, NY), "head": h}


def ring_block(j, zc, d):
    other = lax.rem(j // NY + zc, 2)
    return other * NY + lax.rem(lax.rem(j, NY) + d + 2 * NY, NY)


def all_peers(i, j, h):
    return (
        [head_peer(i, j, h, d) for d in range(1, HEADS)]
        + [x_peer(i, j, h, d) for d in range(1, NX)]
        + [z_peer(i, j, h), y_peer(i, j, h, 1), y_peer(i, j, h, -1)]
    )


def block_positions(spans, x, j):
    lane = lax.broadcasted_iota(jnp.int32, (1, BLOCK), 1)
    at = 2 * (x * NJ + j)
    return jnp.where(lane < CH, spans[at] * CH, spans[at + 1] * CH - CH) + lane


def extra_row(extra_ref, n):
    return jnp.concatenate([extra_ref[8 * x + n : 8 * x + n + 1, :] for x in range(NX)], axis=1)


def masked_scores(spans, starts, qpos, key_block, query_head):
    scores = lax.dot_general(key_block, query_head, NT, preferred_element_type=jnp.float32)
    row = lax.broadcasted_iota(jnp.int32, (CH, QT), 0) - qpos
    parts = [
        jnp.where(row <= -CH * spans[at], scores[n * CH : (n + 1) * CH], LOW)
        for n, at in enumerate(starts)
    ]
    return jnp.concatenate(parts, axis=0)


def attention_kernel(
    spans, q_ref, g_ref, k_ref, v_ref, o_ref, w_ref, oq, ok, ov,
    e_ref, qa, ga, ka, va, ea, ep, st, sa, acc, dq, dk, dv, rq, xs, rr, run, zs, zr, sq, sk, sv,
    local_sem, send1, recv1, send2, recv2, send3, recv3, send4, recv4, send5, recv5,
    send6, recv6, send7, recv7, send8, recv8, send9, recv9, out_sem, send10, recv10,
):
    i, j, h = place()
    zh, core = h // 2, lax.rem(h, 2)
    peers = all_peers(i, j, h)
    announce(peers)

    lane_head = lax.broadcasted_iota(jnp.int32, (8, GROUP * WIDTH), 1) // WIDTH
    pick = (lane_head == lax.broadcasted_iota(jnp.int32, (8, GROUP * WIDTH), 0)).astype(jnp.float32)
    for c in range(KEY_VALUE_HEADS):
        part = slice(c * GROUP * WIDTH, (c + 1) * GROUP * WIDTH)
        product = g_ref[:, part].astype(jnp.float32) * o_ref[:, part].astype(jnp.float32)
        sums = lax.dot_general(
            pick, product, NT, precision=lax.Precision.HIGHEST, preferred_element_type=jnp.float32
        )
        e_ref[8 * c : 8 * c + 8, :] = jnp.concatenate(
            [sums, jnp.zeros((8, 128 - OWN), jnp.float32)], axis=1
        )
    pl.semaphore_wait(pltpu.get_barrier_semaphore(), len(peers))
    sent = []

    def push(src, dst, send, recv, peer):
        copy = remote(src, dst, send, recv, peer)
        copy.start()
        sent.append(copy)
        return copy

    ways = (1, -1)
    x_ways = (1, NX - 1)

    near_first = (1, 2, 3, 6, 7, 4, 5)

    def rank(at):
        return lax.rem(zh + at // 2, 4) * 2 + lax.rem(core + at % 2, 2)

    def pieces(c):
        mine_q = cols(i * HEADS + h, OWN)
        mine_k = cols(j * HEADS + h, OWN)
        return [
            (k_ref.at[:, cols(c, WIDTH)], ka.at[mine_k, :]),
            (v_ref.at[:, cols(c, WIDTH)], va.at[mine_k, :]),
            (e_ref.at[cols(c, 8), :], ep.at[cols(h, 8), :]),
            (q_ref.at[:, cols(c, GROUP * WIDTH)], qa.at[mine_q, :]),
            (g_ref.at[:, cols(c, GROUP * WIDTH)], ga.at[mine_q, :]),
        ]

    first = {}
    for kinds in ((0, 1), (2, 3, 4)):
        for at in near_first:
            c = rank(at)
            for n in kinds:
                src, dst = pieces(c)[n]
                peer = {"ctx": i * NJ + j, "head": c}
                first[at, n] = push(src, dst, send1.at[at, n], recv1.at[at, n], peer)
    own = []
    for n, (src, dst) in enumerate(pieces(h)):
        copy = pltpu.make_async_copy(src, dst, local_sem.at[n])
        copy.start()
        own.append(copy)
    for copy in own:
        copy.wait()

    pair = (ka, va)
    ring = {}

    def spread(ref, rows, send, recv, peer):
        return push(ref.at[rows, :], ref.at[rows, :], send, recv, peer)

    def ring_push(step, zc, way, kinds):
        rows = cols(ring_block(j, zc, -ways[way] * (step - 1)), BLOCK)
        for n in kinds:
            at = (way, step - 1, zc, n)
            ring[way, step, zc, n] = spread(
                pair[n], rows, send3.at[at], recv3.at[at], y_peer(i, j, h, ways[way])
            )

    def ring_step(step):
        for zc in range(2):
            for way in range(2):
                for n in range(2):
                    ring[way, step - 1, zc, n].wait_recv()
                ring_push(step, zc, way, (0, 1) if step < 4 else (way,))

    x_first, x_last = {}, {}

    def x_start(dz):
        for dc in range(2):
            if dz or dc:
                for n in (3, 4):
                    first[2 * dz + dc, n].wait_recv()
        rows = cols(i * 4 + lax.rem(zh - dz + 4, 4), 2 * OWN)
        for way in range(2):
            for n, ref in enumerate((qa, ga)):
                at = (way, 0, n, dz)
                x_first[way, n, dz] = spread(
                    ref, rows, send2.at[at], recv2.at[at], x_peer(i, j, h, x_ways[way])
                )

    def x_relay(dz):
        for way, ref in enumerate((qa, ga)):
            x_first[way, way, dz].wait_recv()
            x = lax.rem(i - ways[way] + NX, NX)
            rows = cols(x * 4 + lax.rem(zh - dz + 4, 4), 2 * OWN)
            at = (way, 1, way, dz)
            x_last[way, dz] = spread(
                ref, rows, send2.at[at], recv2.at[at], x_peer(i, j, h, x_ways[way])
            )

    for n in range(2):
        for at in near_first:
            first[at, n].wait_recv()
    across = [
        spread(pair[n], cols(j, BLOCK), send4.at[n], recv4.at[n], z_peer(i, j, h))
        for n in range(2)
    ]
    for way in range(2):
        ring_push(1, 0, way, (0, 1))
    x_start(0)
    for copy in across:
        copy.wait_recv()
    for way in range(2):
        ring_push(1, 1, way, (0, 1))
    ring_step(2)
    x_start(1)
    x_start(3)
    ring_step(3)
    x_start(2)
    x_relay(0)
    for at in near_first:
        first[at, 2].wait_recv()
    own_extra = jnp.concatenate([ep[8 * n : 8 * n + 8, :OWN] for n in range(HEADS)], axis=1)
    own_gain = w_ref[...].astype(jnp.float32) * 0.25
    extra_at = lax.broadcasted_iota(jnp.int32, (8, BLOCK), 0)
    ea[cols(i, 8), :] = jnp.where(extra_at == GROUP, own_gain, own_extra)
    extras = [
        spread(ea, cols(i, 8), send5.at[d], recv5.at[d], x_peer(i, j, h, d)) for d in range(1, NX)
    ]
    ring_step(4)
    x_relay(1)
    x_relay(3)
    x_relay(2)

    first_span = i * (KT // CH)
    st[...] = jnp.where(
        lax.broadcasted_iota(jnp.int32, (2 * GROUP, QT), 0) < GROUP, FLOOR, jnp.float32(0.0)
    )

    def stats_of(x, couple):
        x_rows = cols(x, BLOCK)
        block = jnp.concatenate(
            [qa[x_rows, g * WIDTH : (g + 1) * WIDTH] for g in range(GROUP)], axis=0
        )
        positions = jnp.concatenate([block_positions(spans, x, j)] * GROUP, axis=1)
        found = [(st[:GROUP, x_rows], st[GROUP:, x_rows])]
        for half in range(2):
            d = (couple + half) * (2 * half - 1)
            owners = [ring_block(j, zc, d) for zc in range(2)]
            key_block = jnp.concatenate([ka[cols(o, BLOCK), :] for o in owners], axis=0)
            starts = [first_span + owner * 2 + n for owner in owners for n in range(2)]
            scores = masked_scores(spans, starts, positions, key_block, block)
            top = jnp.maximum(FLOOR, jnp.max(scores, axis=0, keepdims=True))
            total = jnp.sum(jnp.exp2((scores - top) * SCALE2), axis=0, keepdims=True)
            found.append(
                [
                    jnp.concatenate(
                        [r[:, g * BLOCK : (g + 1) * BLOCK] for g in range(GROUP)], axis=0
                    )
                    for r in (top, total)
                ]
            )
        top = functools.reduce(jnp.maximum, [r[0] for r in found])
        st[:GROUP, x_rows] = top
        st[GROUP:, x_rows] = sum(r[1] * jnp.exp2((r[0] - top) * SCALE2) for r in found)

    for dz in range(4):
        x_first[1, 0, dz].wait_recv()

    def near_x(t, carry):
        at = t // 3
        stats_of(lax.rem(i + 3 * at - at // 2, NX), lax.rem(t, 3))
        return carry

    def far_x(t, carry):
        stats_of(lax.rem(i + 2, NX), t)
        return carry

    def far_y(t, carry):
        stats_of(t, 3)
        return carry

    lax.fori_loop(0, 9, near_x, 0)
    for dz in range(4):
        x_last[0, dz].wait_recv()
    lax.fori_loop(0, 3, far_x, 0)
    for zc in range(2):
        for way in range(2):
            ring[way, 4, zc, way].wait_recv()
    lax.fori_loop(0, 4, far_y, 0)
    shared = [
        push(st, sa.at[d - 1], send6.at[d], recv6.at[d], x_peer(i, j, h, d)) for d in range(1, NX)
    ]
    for dz in range(4):
        x_first[0, 1, dz].wait_recv()
        x_last[1, dz].wait_recv()
    for copy in extras:
        copy.wait_recv()
    qpos = jnp.concatenate([block_positions(spans, x, j) for x in range(NX)], axis=1)
    gain = extra_row(ea, GROUP)
    gain_scale = gain * SCALE
    out_dots = [extra_row(ea, g) for g in range(GROUP)]
    acc[...] = jnp.zeros_like(acc)
    for copy in shared:
        copy.wait_recv()
    blocks = [st[...]] + [sa[d] for d in range(NX - 1)]
    top = functools.reduce(jnp.maximum, [b[:GROUP] for b in blocks])
    total = sum(b[GROUP:] * jnp.exp2((b[:GROUP] - top) * SCALE2) for b in blocks)
    norm_rows = top * SCALE2 + jnp.log2(total)
    norms = [norm_rows[g : g + 1] for g in range(GROUP)]

    query_parts = {}

    def x_to(way):
        return cols(lax.rem(i + x_ways[way], NX), BLOCK)

    def x_push(src, way, step, g):
        query_parts[way, step, g] = push(
            src,
            rq.at[way, step, g],
            send8.at[way, step, g],
            recv8.at[way, step, g],
            x_peer(i, j, h, x_ways[way]),
        )

    def x_add(g):
        way = g // 2
        query_parts[way, 0, g].wait_recv()
        total = dq[g, x_to(way), :].astype(jnp.float32) + rq[way, 0, g].astype(jnp.float32)
        xs[g] = total.astype(jnp.bfloat16)
        x_push(xs.at[g], way, 1, g)

    def grads_of(distances, closing=False):
        owners = [ring_block(j, zc, d) for d in distances for zc in range(2)]
        rows = [cols(owner, BLOCK) for owner in owners]
        key_block = jnp.concatenate([ka[r, :] for r in rows], axis=0)
        value_block = jnp.concatenate([va[r, :] for r in rows], axis=0)
        starts = [first_span + owner * 2 + n for owner in owners for n in range(2)]
        key_grad = jnp.zeros((len(owners) * BLOCK, WIDTH), jnp.float32)
        value_grad = jnp.zeros((len(owners) * BLOCK, WIDTH), jnp.float32)
        for g in range(GROUP):
            part = slice(g * WIDTH, (g + 1) * WIDTH)
            query_head = qa[:, part]
            grad_head = ga[:, part]
            scores = masked_scores(spans, starts, qpos, key_block, query_head)
            probs = jnp.exp2(scores * SCALE2 - norms[g])
            prob_grads = lax.dot_general(
                value_block, grad_head, NT, preferred_element_type=jnp.float32
            )
            weighted = (probs * gain).astype(jnp.bfloat16)
            score_grads = (probs * ((prob_grads - out_dots[g]) * gain_scale)).astype(jnp.bfloat16)
            query_term = lax.dot_general(
                score_grads, key_block, TN, preferred_element_type=jnp.float32
            )
            if closing:
                dq[g] = (acc[:, part] + query_term).astype(jnp.bfloat16)
                way = g // 2
                x_push(dq.at[g, cols(lax.rem(i + 2, NX), BLOCK), :], way, 0, g)
                x_push(dq.at[g, x_to(1 - way), :], 1 - way, 1, g)
            else:
                acc[:, part] += query_term
            key_grad += jnp.dot(score_grads, query_head, preferred_element_type=jnp.float32)
            value_grad += jnp.dot(weighted, grad_head, preferred_element_type=jnp.float32)
        for n, r in enumerate(rows):
            dk[r, :] = key_grad[n * BLOCK : (n + 1) * BLOCK].astype(jnp.bfloat16)
            dv[r, :] = value_grad[n * BLOCK : (n + 1) * BLOCK].astype(jnp.bfloat16)

    partial = (dk, dv)
    back = {}

    def back_push(src, way, step, zc, n):
        at = (way, step - 1, zc, n)
        back[way, step, zc, n] = push(
            src, rr.at[at], send7.at[at], recv7.at[at], y_peer(i, j, h, ways[way])
        )

    def target(way, step, zc):
        return cols(ring_block(j, zc, ways[way] * (5 - step)), BLOCK)

    def back_step(way, step):
        for zc in (1, 0):
            if step == 2:
                src = partial[1 - way].at[target(way, 2, zc), :]
                back_push(src, way, 2, zc, 1 - way)
            for n in range(2) if step > 2 else (way,):
                back[way, step - 1, zc, n].wait_recv()
                total = rr[way, step - 2, zc, n].astype(jnp.float32) + partial[n][
                    target(way, step, zc), :
                ].astype(jnp.float32)
                run[way, step - 2, zc, n] = total.astype(jnp.bfloat16)
                back_push(run.at[way, step - 2, zc, n], way, step, zc, n)

    grads_of((4,))
    for zc in (1, 0):
        for way in range(2):
            back_push(partial[way].at[target(way, 1, zc), :], way, 1, zc, way)
    for step in range(2, 5):
        for way in range(2):
            grads_of((ways[way] * (5 - step),))
            back_step(way, step)
    grads_of((0,), closing=True)
    for g in range(GROUP):
        x_add(g)

    def ring_total(zc, n):
        for way in range(2):
            back[way, 4, zc, n].wait_recv()
        rows = cols(ring_block(j, zc, 0), BLOCK)
        return (
            partial[n][rows, :].astype(jnp.float32)
            + rr[0, 3, zc, n].astype(jnp.float32)
            + rr[1, 3, zc, n].astype(jnp.float32)
        )

    last, kept = [], []

    def give(n, source, out):
        for at in (4, 5, 2, 3, 6, 7, 1):
            c = rank(at)
            peer = {"ctx": i * NJ + j, "head": c}
            src = source.at[cols(c, OWN), :]
            last.append(push(src, out, send10.at[at, n], recv10.at[at, n], peer))
        copy = pltpu.make_async_copy(source.at[cols(h, OWN), :], out, out_sem.at[n])
        copy.start()
        kept.append(copy)

    def give_queries(g):
        total = dq[g, cols(i, BLOCK), :].astype(jnp.float32)
        for way in range(2):
            query_parts[way, 1, g].wait_recv()
            total += rq[way, 1, g].astype(jnp.float32)
        sq[g] = total.astype(jnp.bfloat16)
        give(g, sq.at[g], oq.at[:, cols(h * GROUP + g, WIDTH)])

    over = []
    for n in range(2):
        zs[n] = ring_total(1, n).astype(jnp.bfloat16)
        over.append(push(zs.at[n], zr.at[n], send9.at[n], recv9.at[n], z_peer(i, j, h)))
    give_queries(0)
    give_queries(1)
    for n, (held, out) in enumerate(((sk, ok), (sv, ov))):
        total = ring_total(0, n)
        over[n].wait_recv()
        held[...] = (total + zr[n].astype(jnp.float32)).astype(jnp.bfloat16)
        give(GROUP + n, held, out.at[:, cols(h, WIDTH)])
    give_queries(2)
    give_queries(3)
    for copy in kept:
        copy.wait()
    for copy in last:
        copy.wait_recv()
    for copy in sent:
        copy.wait_send()


def attention(spans, queries, grads, keys, values, outputs, importance):
    dma = pltpu.SemaphoreType.DMA
    bf16, f32 = jnp.bfloat16, jnp.float32
    vmem = pltpu.VMEM

    def both(*shape):
        return [dma(shape), dma(shape)]

    return pl.pallas_call(
        attention_kernel,
        out_shape=(
            jax.ShapeDtypeStruct((OWN, QUERY_HEADS * WIDTH), bf16),
            jax.ShapeDtypeStruct((OWN, KEY_VALUE_HEADS * WIDTH), bf16),
            jax.ShapeDtypeStruct((OWN, KEY_VALUE_HEADS * WIDTH), bf16),
        ),
        in_specs=[SMEM] + [VMEM] * 6,
        out_specs=[VMEM] * 3,
        scratch_shapes=[
            vmem((KEY_VALUE_HEADS * 8, 128), f32),
            vmem((QT, GROUP * WIDTH), bf16),
            vmem((QT, GROUP * WIDTH), bf16),
            vmem((KT, WIDTH), bf16),
            vmem((KT, WIDTH), bf16),
            vmem((NX * 8, 128), f32),
            vmem((HEADS * 8, 128), f32),
            vmem((2 * GROUP, QT), f32),
            vmem((NX - 1, 2 * GROUP, QT), f32),
            vmem((QT, GROUP * WIDTH), f32),
            vmem((GROUP, QT, WIDTH), bf16),
            vmem((KT, WIDTH), bf16),
            vmem((KT, WIDTH), bf16),
            vmem((2, 2, GROUP, BLOCK, WIDTH), bf16),
            vmem((GROUP, BLOCK, WIDTH), bf16),
            vmem((2, 4, 2, 2, BLOCK, WIDTH), bf16),
            vmem((2, 3, 2, 2, BLOCK, WIDTH), bf16),
            vmem((2, BLOCK, WIDTH), bf16),
            vmem((2, BLOCK, WIDTH), bf16),
            vmem((GROUP, BLOCK, WIDTH), bf16),
            vmem((BLOCK, WIDTH), bf16),
            vmem((BLOCK, WIDTH), bf16),
            dma((5,)),
        ]
        + both(HEADS, 5)
        + both(2, 2, 2, 4)
        + both(2, 4, 2, 2)
        + both(2)
        + both(NX)
        + both(NX)
        + both(2, 4, 2, 2)
        + both(2, 2, GROUP)
        + both(2)
        + [dma((GROUP + 2,))]
        + both(HEADS, GROUP + 2),
        compiler_params=pltpu.CompilerParams(collective_id=0, has_side_effects=True),
        name="attention",
    )(spans, queries, grads, keys, values, outputs, importance)


def on_device(queries, keys, values, outputs, output_gradient, importance, span_order):
    return attention(
        span_order, queries, output_gradient, keys, values, outputs, importance.reshape(1, BLOCK)
    )


def solution(mesh):
    tokens = P(("ctx", "head"), None)
    return jax.shard_map(
        on_device,
        mesh=mesh,
        in_specs=(tokens, tokens, tokens, tokens, tokens, P("ctx"), P()),
        out_specs=(tokens, tokens, tokens),
        check_vma=False,
    )
```

```python
import functools
import math

import jax
import jax.numpy as jnp
from jax import lax
from jax.experimental import pallas as pl
from jax.experimental.pallas import tpu as pltpu
from jax.sharding import PartitionSpec as P

QUERY_HEADS = 32
KEY_VALUE_HEADS = 8
GROUP = 4
WIDTH = 128
CH = 64
HEADS = 8
NX = 4
NJ = 16
NY = 8
OWN = 16
BLOCK = 128
QT = NX * BLOCK
KT = NJ * BLOCK
KB = 512
SCALE = 1.0 / math.sqrt(WIDTH)
SCALE2 = SCALE * math.log2(math.e)
LOW = -1e30
FLOOR = -1e20

MESH = pl.DeviceIdType.MESH
VMEM = pl.BlockSpec(memory_space=pltpu.VMEM)
SMEM = pl.BlockSpec(memory_space=pltpu.SMEM)
NT = (((1,), (1,)), ((), ()))
TN = (((0,), (0,)), ((), ()))


def place():
    ctx = lax.axis_index("ctx")
    return ctx // NJ, lax.rem(ctx, NJ), lax.axis_index("head")


def head_peer(i, j, h, d):
    return {"ctx": i * NJ + j, "head": lax.rem(h + d, HEADS)}


def x_peer(i, j, h, d):
    return {"ctx": lax.rem(i + d, NX) * NJ + j, "head": h}


def announce(peers):
    for peer in peers:
        pl.semaphore_signal(
            pltpu.get_barrier_semaphore(), inc=1, device_id=peer, device_id_type=MESH
        )


def remote(src, dst, send, recv, peer):
    return pltpu.make_async_remote_copy(
        src_ref=src, dst_ref=dst, send_sem=send, recv_sem=recv, device_id=peer, device_id_type=MESH
    )


def cols(index, width):
    return pl.ds(pl.multiple_of(index * width, width), width)


def z_peer(i, j, h):
    return {"ctx": i * NJ + lax.rem(j + NY, NJ), "head": h}


def y_peer(i, j, h, d):
    return {"ctx": i * NJ + (j // NY) * NY + lax.rem(lax.rem(j, NY) + d + NY, NY), "head": h}


def ring_block(j, zc, d):
    other = lax.rem(j // NY + zc, 2)
    return other * NY + lax.rem(lax.rem(j, NY) + d + 2 * NY, NY)


def all_peers(i, j, h):
    return (
        [head_peer(i, j, h, d) for d in range(1, HEADS)]
        + [x_peer(i, j, h, d) for d in range(1, NX)]
        + [z_peer(i, j, h), y_peer(i, j, h, 1), y_peer(i, j, h, -1)]
    )


def block_positions(spans, x, j):
    lane = lax.broadcasted_iota(jnp.int32, (1, BLOCK), 1)
    at = 2 * (x * NJ + j)
    return jnp.where(lane < CH, spans[at] * CH, spans[at + 1] * CH - CH) + lane


def extra_row(extra_ref, n):
    return jnp.concatenate([extra_ref[8 * x + n : 8 * x + n + 1, :] for x in range(NX)], axis=1)


def masked_scores(spans, starts, qpos, key_block, query_head):
    scores = lax.dot_general(key_block, query_head, NT, preferred_element_type=jnp.float32)
    row = lax.broadcasted_iota(jnp.int32, (CH, QT), 0) - qpos
    parts = [
        jnp.where(row <= -CH * spans[at], scores[n * CH : (n + 1) * CH], LOW)
        for n, at in enumerate(starts)
    ]
    return jnp.concatenate(parts, axis=0)


def attention_kernel(
    spans, q_ref, g_ref, k_ref, v_ref, o_ref, w_ref, oq, ok, ov,
    e_ref, qa, ga, ka, va, ea, ep, st, sa, acc, dq, dk, dv, rq, rr, run, zs, zr, sq, sk, sv,
    local_sem, send1, recv1, send2, recv2, send3, recv3, send4, recv4, send5, recv5,
    send6, recv6, send7, recv7, send8, recv8, send9, recv9, out_sem, send10, recv10,
):
    i, j, h = place()
    zh, core = h // 2, lax.rem(h, 2)
    peers = all_peers(i, j, h)
    announce(peers)

    lane_head = lax.broadcasted_iota(jnp.int32, (8, GROUP * WIDTH), 1) // WIDTH
    pick = (lane_head == lax.broadcasted_iota(jnp.int32, (8, GROUP * WIDTH), 0)).astype(jnp.float32)
    for c in range(KEY_VALUE_HEADS):
        part = slice(c * GROUP * WIDTH, (c + 1) * GROUP * WIDTH)
        product = g_ref[:, part].astype(jnp.float32) * o_ref[:, part].astype(jnp.float32)
        sums = lax.dot_general(
            pick, product, NT, precision=lax.Precision.HIGHEST, preferred_element_type=jnp.float32
        )
        e_ref[8 * c : 8 * c + 8, :] = jnp.concatenate(
            [sums, jnp.zeros((8, 128 - OWN), jnp.float32)], axis=1
        )
    pl.semaphore_wait(pltpu.get_barrier_semaphore(), len(peers))
    sent = []

    def push(src, dst, send, recv, peer):
        copy = remote(src, dst, send, recv, peer)
        copy.start()
        sent.append(copy)
        return copy

    ways = (1, -1)
    x_ways = (1, NX - 1)

    near_first = (1, 2, 3, 6, 7, 4, 5)

    def rank(at):
        return lax.rem(zh + at // 2, 4) * 2 + lax.rem(core + at % 2, 2)

    def pieces(c):
        mine_q = cols(i * HEADS + h, OWN)
        mine_k = cols(j * HEADS + h, OWN)
        return [
            (k_ref.at[:, cols(c, WIDTH)], ka.at[mine_k, :]),
            (v_ref.at[:, cols(c, WIDTH)], va.at[mine_k, :]),
            (e_ref.at[cols(c, 8), :], ep.at[cols(h, 8), :]),
            (q_ref.at[:, cols(c, GROUP * WIDTH)], qa.at[mine_q, :]),
            (g_ref.at[:, cols(c, GROUP * WIDTH)], ga.at[mine_q, :]),
        ]

    first = {}
    for kinds in ((0, 1), (2, 3, 4)):
        for at in near_first:
            c = rank(at)
            for n in kinds:
                src, dst = pieces(c)[n]
                peer = {"ctx": i * NJ + j, "head": c}
                first[at, n] = push(src, dst, send1.at[at, n], recv1.at[at, n], peer)
    own = []
    for n, (src, dst) in enumerate(pieces(h)):
        copy = pltpu.make_async_copy(src, dst, local_sem.at[n])
        copy.start()
        own.append(copy)
    for copy in own:
        copy.wait()

    pair = (ka, va)
    ring = {}

    def spread(ref, rows, send, recv, peer):
        return push(ref.at[rows, :], ref.at[rows, :], send, recv, peer)

    def ring_push(step, zc, way, kinds):
        rows = cols(ring_block(j, zc, -ways[way] * (step - 1)), BLOCK)
        for n in kinds:
            at = (way, step - 1, zc, n)
            ring[way, step, zc, n] = spread(
                pair[n], rows, send3.at[at], recv3.at[at], y_peer(i, j, h, ways[way])
            )

    def ring_step(step):
        for zc in range(2):
            for way in range(2):
                for n in range(2):
                    ring[way, step - 1, zc, n].wait_recv()
                ring_push(step, zc, way, (0, 1) if step < 4 else (way,))

    x_first, x_last = {}, {}

    def x_start(dz):
        for dc in range(2):
            if dz or dc:
                for n in (3, 4):
                    first[2 * dz + dc, n].wait_recv()
        rows = cols(i * 4 + lax.rem(zh - dz + 4, 4), 2 * OWN)
        for way in range(2):
            for n, ref in enumerate((qa, ga)):
                at = (way, 0, n, dz)
                x_first[way, n, dz] = spread(
                    ref, rows, send2.at[at], recv2.at[at], x_peer(i, j, h, x_ways[way])
                )

    def x_relay(dz):
        for way, ref in enumerate((qa, ga)):
            x_first[way, way, dz].wait_recv()
            x = lax.rem(i - ways[way] + NX, NX)
            rows = cols(x * 4 + lax.rem(zh - dz + 4, 4), 2 * OWN)
            at = (way, 1, way, dz)
            x_last[way, dz] = spread(
                ref, rows, send2.at[at], recv2.at[at], x_peer(i, j, h, x_ways[way])
            )

    for n in range(2):
        for at in near_first:
            first[at, n].wait_recv()
    across = [
        spread(pair[n], cols(j, BLOCK), send4.at[n], recv4.at[n], z_peer(i, j, h))
        for n in range(2)
    ]
    for way in range(2):
        ring_push(1, 0, way, (0, 1))
    x_start(0)
    for copy in across:
        copy.wait_recv()
    for way in range(2):
        ring_push(1, 1, way, (0, 1))
    ring_step(2)
    x_start(1)
    x_start(3)
    ring_step(3)
    x_start(2)
    x_relay(0)
    for at in near_first:
        first[at, 2].wait_recv()
    own_extra = jnp.concatenate([ep[8 * n : 8 * n + 8, :OWN] for n in range(HEADS)], axis=1)
    own_gain = w_ref[...].astype(jnp.float32) * 0.25
    extra_at = lax.broadcasted_iota(jnp.int32, (8, BLOCK), 0)
    ea[cols(i, 8), :] = jnp.where(extra_at == GROUP, own_gain, own_extra)
    extras = [
        spread(ea, cols(i, 8), send5.at[d], recv5.at[d], x_peer(i, j, h, d)) for d in range(1, NX)
    ]
    ring_step(4)
    x_relay(1)
    x_relay(3)
    x_relay(2)

    first_span = i * (KT // CH)
    st[...] = jnp.where(
        lax.broadcasted_iota(jnp.int32, (2 * GROUP, QT), 0) < GROUP, FLOOR, jnp.float32(0.0)
    )

    def stats_of(x, couple):
        x_rows = cols(x, BLOCK)
        block = jnp.concatenate(
            [qa[x_rows, g * WIDTH : (g + 1) * WIDTH] for g in range(GROUP)], axis=0
        )
        positions = jnp.concatenate([block_positions(spans, x, j)] * GROUP, axis=1)
        found = [(st[:GROUP, x_rows], st[GROUP:, x_rows])]
        for half in range(2):
            d = (couple + half) * (2 * half - 1)
            owners = [ring_block(j, zc, d) for zc in range(2)]
            key_block = jnp.concatenate([ka[cols(o, BLOCK), :] for o in owners], axis=0)
            starts = [first_span + owner * 2 + n for owner in owners for n in range(2)]
            scores = masked_scores(spans, starts, positions, key_block, block)
            top = jnp.maximum(FLOOR, jnp.max(scores, axis=0, keepdims=True))
            total = jnp.sum(jnp.exp2((scores - top) * SCALE2), axis=0, keepdims=True)
            found.append(
                [
                    jnp.concatenate(
                        [r[:, g * BLOCK : (g + 1) * BLOCK] for g in range(GROUP)], axis=0
                    )
                    for r in (top, total)
                ]
            )
        top = functools.reduce(jnp.maximum, [r[0] for r in found])
        st[:GROUP, x_rows] = top
        st[GROUP:, x_rows] = sum(r[1] * jnp.exp2((r[0] - top) * SCALE2) for r in found)

    for dz in range(4):
        x_first[1, 0, dz].wait_recv()

    def near_x(t, carry):
        at = t // 3
        stats_of(lax.rem(i + 3 * at - at // 2, NX), lax.rem(t, 3))
        return carry

    def far_x(t, carry):
        stats_of(lax.rem(i + 2, NX), t)
        return carry

    def far_y(t, carry):
        stats_of(t, 3)
        return carry

    lax.fori_loop(0, 9, near_x, 0)
    for dz in range(4):
        x_last[0, dz].wait_recv()
    lax.fori_loop(0, 3, far_x, 0)
    for zc in range(2):
        for way in range(2):
            ring[way, 4, zc, way].wait_recv()
    lax.fori_loop(0, 4, far_y, 0)
    shared = [
        push(st, sa.at[d - 1], send6.at[d], recv6.at[d], x_peer(i, j, h, d)) for d in range(1, NX)
    ]
    for dz in range(4):
        x_first[0, 1, dz].wait_recv()
        x_last[1, dz].wait_recv()
    for copy in extras:
        copy.wait_recv()
    qpos = jnp.concatenate([block_positions(spans, x, j) for x in range(NX)], axis=1)
    gain = extra_row(ea, GROUP)
    gain_scale = gain * SCALE
    out_dots = [extra_row(ea, g) for g in range(GROUP)]
    acc[...] = jnp.zeros_like(acc)
    for copy in shared:
        copy.wait_recv()
    blocks = [st[...]] + [sa[d] for d in range(NX - 1)]
    top = functools.reduce(jnp.maximum, [b[:GROUP] for b in blocks])
    total = sum(b[GROUP:] * jnp.exp2((b[:GROUP] - top) * SCALE2) for b in blocks)
    norm_rows = top * SCALE2 + jnp.log2(total)
    norms = [norm_rows[g : g + 1] for g in range(GROUP)]

    query_parts = {}

    def grads_of(distances, closing=False):
        owners = [ring_block(j, zc, d) for d in distances for zc in range(2)]
        rows = [cols(owner, BLOCK) for owner in owners]
        key_block = jnp.concatenate([ka[r, :] for r in rows], axis=0)
        value_block = jnp.concatenate([va[r, :] for r in rows], axis=0)
        starts = [first_span + owner * 2 + n for owner in owners for n in range(2)]
        key_grad = jnp.zeros((len(owners) * BLOCK, WIDTH), jnp.float32)
        value_grad = jnp.zeros((len(owners) * BLOCK, WIDTH), jnp.float32)
        for g in range(GROUP):
            part = slice(g * WIDTH, (g + 1) * WIDTH)
            query_head = qa[:, part]
            grad_head = ga[:, part]
            scores = masked_scores(spans, starts, qpos, key_block, query_head)
            probs = jnp.exp2(scores * SCALE2 - norms[g])
            prob_grads = lax.dot_general(
                value_block, grad_head, NT, preferred_element_type=jnp.float32
            )
            weighted = (probs * gain).astype(jnp.bfloat16)
            score_grads = (probs * ((prob_grads - out_dots[g]) * gain_scale)).astype(jnp.bfloat16)
            query_term = lax.dot_general(
                score_grads, key_block, TN, preferred_element_type=jnp.float32
            )
            if closing:
                dq[g] = (acc[:, part] + query_term).astype(jnp.bfloat16)
                for d in range(1, NX):
                    query_parts[d, g] = push(
                        dq.at[g, cols(lax.rem(i + d, NX), BLOCK), :],
                        rq.at[d - 1, g],
                        send8.at[d, g],
                        recv8.at[d, g],
                        x_peer(i, j, h, d),
                    )
            else:
                acc[:, part] += query_term
            key_grad += jnp.dot(score_grads, query_head, preferred_element_type=jnp.float32)
            value_grad += jnp.dot(weighted, grad_head, preferred_element_type=jnp.float32)
        for n, r in enumerate(rows):
            dk[r, :] = key_grad[n * BLOCK : (n + 1) * BLOCK].astype(jnp.bfloat16)
            dv[r, :] = value_grad[n * BLOCK : (n + 1) * BLOCK].astype(jnp.bfloat16)

    partial = (dk, dv)
    back = {}

    def back_push(src, way, step, zc, n):
        at = (way, step - 1, zc, n)
        back[way, step, zc, n] = push(
            src, rr.at[at], send7.at[at], recv7.at[at], y_peer(i, j, h, ways[way])
        )

    def target(way, step, zc):
        return cols(ring_block(j, zc, ways[way] * (5 - step)), BLOCK)

    def back_step(way, step):
        for zc in (1, 0):
            if step == 2:
                src = partial[1 - way].at[target(way, 2, zc), :]
                back_push(src, way, 2, zc, 1 - way)
            for n in range(2) if step > 2 else (way,):
                back[way, step - 1, zc, n].wait_recv()
                total = rr[way, step - 2, zc, n].astype(jnp.float32) + partial[n][
                    target(way, step, zc), :
                ].astype(jnp.float32)
                run[way, step - 2, zc, n] = total.astype(jnp.bfloat16)
                back_push(run.at[way, step - 2, zc, n], way, step, zc, n)

    grads_of((4,))
    for zc in (1, 0):
        for way in range(2):
            back_push(partial[way].at[target(way, 1, zc), :], way, 1, zc, way)
    for step in (2, 3):
        for way in range(2):
            grads_of((ways[way] * (5 - step),))
            back_step(way, step)
    grads_of((1,))
    back_step(0, 4)
    grads_of((-1, 0), closing=True)
    back_step(1, 4)

    def ring_total(zc, n):
        for way in range(2):
            back[way, 4, zc, n].wait_recv()
        rows = cols(ring_block(j, zc, 0), BLOCK)
        return (
            partial[n][rows, :].astype(jnp.float32)
            + rr[0, 3, zc, n].astype(jnp.float32)
            + rr[1, 3, zc, n].astype(jnp.float32)
        )

    last, kept = [], []

    def give(n, source, out):
        for at in (4, 5, 2, 3, 6, 7, 1):
            c = rank(at)
            peer = {"ctx": i * NJ + j, "head": c}
            src = source.at[cols(c, OWN), :]
            last.append(push(src, out, send10.at[at, n], recv10.at[at, n], peer))
        copy = pltpu.make_async_copy(source.at[cols(h, OWN), :], out, out_sem.at[n])
        copy.start()
        kept.append(copy)

    def give_queries(g):
        total = dq[g, cols(i, BLOCK), :].astype(jnp.float32)
        for d in range(1, NX):
            query_parts[d, g].wait_recv()
            total += rq[d - 1, g].astype(jnp.float32)
        sq[g] = total.astype(jnp.bfloat16)
        give(g, sq.at[g], oq.at[:, cols(h * GROUP + g, WIDTH)])

    give_queries(0)
    over = []
    for n in range(2):
        zs[n] = ring_total(1, n).astype(jnp.bfloat16)
        over.append(push(zs.at[n], zr.at[n], send9.at[n], recv9.at[n], z_peer(i, j, h)))
    give_queries(1)
    give_queries(2)
    for n, (held, out) in enumerate(((sk, ok), (sv, ov))):
        total = ring_total(0, n)
        over[n].wait_recv()
        held[...] = (total + zr[n].astype(jnp.float32)).astype(jnp.bfloat16)
        give(GROUP + n, held, out.at[:, cols(h, WIDTH)])
    give_queries(3)
    for copy in kept:
        copy.wait()
    for copy in last:
        copy.wait_recv()
    for copy in sent:
        copy.wait_send()


def attention(spans, queries, grads, keys, values, outputs, importance):
    dma = pltpu.SemaphoreType.DMA
    bf16, f32 = jnp.bfloat16, jnp.float32
    vmem = pltpu.VMEM

    def both(*shape):
        return [dma(shape), dma(shape)]

    return pl.pallas_call(
        attention_kernel,
        out_shape=(
            jax.ShapeDtypeStruct((OWN, QUERY_HEADS * WIDTH), bf16),
            jax.ShapeDtypeStruct((OWN, KEY_VALUE_HEADS * WIDTH), bf16),
            jax.ShapeDtypeStruct((OWN, KEY_VALUE_HEADS * WIDTH), bf16),
        ),
        in_specs=[SMEM] + [VMEM] * 6,
        out_specs=[VMEM] * 3,
        scratch_shapes=[
            vmem((KEY_VALUE_HEADS * 8, 128), f32),
            vmem((QT, GROUP * WIDTH), bf16),
            vmem((QT, GROUP * WIDTH), bf16),
            vmem((KT, WIDTH), bf16),
            vmem((KT, WIDTH), bf16),
            vmem((NX * 8, 128), f32),
            vmem((HEADS * 8, 128), f32),
            vmem((2 * GROUP, QT), f32),
            vmem((NX - 1, 2 * GROUP, QT), f32),
            vmem((QT, GROUP * WIDTH), f32),
            vmem((GROUP, QT, WIDTH), bf16),
            vmem((KT, WIDTH), bf16),
            vmem((KT, WIDTH), bf16),
            vmem((NX - 1, GROUP, BLOCK, WIDTH), bf16),
            vmem((2, 4, 2, 2, BLOCK, WIDTH), bf16),
            vmem((2, 3, 2, 2, BLOCK, WIDTH), bf16),
            vmem((2, BLOCK, WIDTH), bf16),
            vmem((2, BLOCK, WIDTH), bf16),
            vmem((GROUP, BLOCK, WIDTH), bf16),
            vmem((BLOCK, WIDTH), bf16),
            vmem((BLOCK, WIDTH), bf16),
            dma((5,)),
        ]
        + both(HEADS, 5)
        + both(2, 2, 2, 4)
        + both(2, 4, 2, 2)
        + both(2)
        + both(NX)
        + both(NX)
        + both(2, 4, 2, 2)
        + both(NX, GROUP)
        + both(2)
        + [dma((GROUP + 2,))]
        + both(HEADS, GROUP + 2),
        compiler_params=pltpu.CompilerParams(collective_id=0, has_side_effects=True),
        name="attention",
    )(spans, queries, grads, keys, values, outputs, importance)


def on_device(queries, keys, values, outputs, output_gradient, importance, span_order):
    return attention(
        span_order, queries, output_gradient, keys, values, outputs, importance.reshape(1, BLOCK)
    )


def solution(mesh):
    tokens = P(("ctx", "head"), None)
    return jax.shard_map(
        on_device,
        mesh=mesh,
        in_specs=(tokens, tokens, tokens, tokens, tokens, P("ctx"), P()),
        out_specs=(tokens, tokens, tokens),
        check_vma=False,
    )
```
